256 devices in a mesh: leaf: 32 (over z, x), rank: 4 (over y), rhs: 2 (over core).
Axes of the slice: x: 4, y: 4, z: 8, core: 2. Of those that a mesh axis runs over, the one named last changes fastest.
Arguments:
- rhs: float32 [65536, 512], P(('leaf', 'rank'), 'rhs'), parts along dimension 1, may hold values from -40 to 40
- order: int32 [65536], P(('leaf', 'rank')), may hold values from 0 to 65535, as said below
- diag: float32 [65536], P(('leaf', 'rank')), may hold values from 2 to 8
- blocks: bfloat16 [1536, 128, 128], P(('leaf', 'rank')), may hold values from -0.3125 to 0.3125
- near_rows: int32 [1536], P(('leaf', 'rank')), may hold values from 0 to 511, as said below
- near_cols: int32 [1536], P(('leaf', 'rank')), may hold values from 0 to 511, as said below
- gen_u: bfloat16 [5, 65536, 128], P(None, 'leaf', 'rank'), may hold values from -0.5 to 0.5
- gen_v: bfloat16 [5, 65536, 128], P(None, 'leaf', 'rank'), may hold values from -0.03125 to 0.03125
Outputs:
- solution: float32 [65536, 512], P(('leaf', 'rank'), 'rhs'), parts along dimension 1
- residual: float32 [65536, 512], P(('leaf', 'rank'), 'rhs'), parts along dimension 1
The draws below stay inside these ranges and needn't reach their ends.
There are 2 independent parts, one for each index of `rhs`. The reference program is written for one: setup_inputs(seed, part) draws one part's arguments, and reference() takes and returns one part's arrays. A program takes and returns all parts, laid end to end along the dimension named above; an argument that names none is the same for every part. Nothing has to cross between parts.
Inputs may be any that keep to these rules, and one draw needn't show every extreme that they name: `order`: each aligned run of 512 entries is a permutation of the panel numbers of that run. `near_rows`: block k's row is one of the 4 block rows of the device that holds block k; every block row is named, at least once by a block whose column equals it. `near_cols`: block k's column lies in the same subtree of 2048 panels as its row, at most 4 block columns away from it.
All inputs are finite; a program needn't handle non-finite values.
Results may differ from the reference program's by a relative error of at most 0.0035.
Values may be sent and summed in bfloat16 or wider, within the bound.
A program may use at most 64 MiB of HBM per device.

```python
import math
import jax
import jax.numpy as jnp
from jax import lax

BLK = 128
K = 128
NRHS = 256
NEAR_ROW = 3
PAN_LEAF = 2048
PAN_DEV = 512
NPAN = 65536
NBLK = 1536
LEVELS = 5


def near_pattern(key):
    rows_dev = PAN_DEV // BLK
    per_dev = NEAR_ROW * rows_dev
    rows_leaf = PAN_LEAF // BLK
    devices = NPAN // PAN_DEV
    ranks = PAN_LEAF // PAN_DEV
    key_row, key_off, key_mix = jax.random.split(jax.random.fold_in(key, 7), 3)
    position = jnp.arange(per_dev, dtype=jnp.int32)[None, :]
    device = jnp.arange(devices, dtype=jnp.int32)[:, None]
    extra = jax.random.randint(key_row, (devices, per_dev), 0, rows_dev, dtype=jnp.int32)
    local_row = jnp.where(position < rows_dev, position, extra)
    offset = jax.random.randint(key_off, (devices, per_dev), -4, 5, dtype=jnp.int32)
    offset = jnp.where(position < rows_dev, 0, offset)
    global_row = device * rows_dev + local_row
    leaf_start = device // ranks * rows_leaf
    column = leaf_start + jnp.clip(global_row - leaf_start + offset, 0, rows_leaf - 1)
    scores = jax.random.randint(key_mix, (devices, per_dev), 0, 1 << 16, dtype=jnp.int32) * per_dev + position
    mixing = jnp.argsort(scores, axis=1, stable=True).astype(jnp.int32)
    rows = jnp.take_along_axis(global_row, mixing, axis=1).reshape(-1).astype(jnp.int32)
    cols = jnp.take_along_axis(column, mixing, axis=1).reshape(-1).astype(jnp.int32)
    return (rows, cols)


def draw_near_rows(key, part):
    return near_pattern(key)[0]


def draw_near_cols(key, part):
    return near_pattern(key)[1]


def draw_order(key, part):
    devices = NPAN // PAN_DEV
    position = jnp.arange(PAN_DEV, dtype=jnp.int32)[None, :]
    device = jnp.arange(devices, dtype=jnp.int32)[:, None]
    scores = jax.random.randint(jax.random.fold_in(key, 13), (devices, PAN_DEV), 0, 1 << 12, dtype=jnp.int32) * PAN_DEV + position
    mixing = jnp.argsort(scores, axis=1, stable=True).astype(jnp.int32)
    return (device * PAN_DEV + mixing).reshape(-1).astype(jnp.int32)


def draw_rhs(key, part):
    key_scale, key_entry = jax.random.split(jax.random.fold_in(key, 11), 2)
    position = jnp.arange(NPAN, dtype=jnp.float32)
    ramp = 1.0 + 2.0 * position / max(NPAN - 1, 1)
    spread = jnp.exp(jax.random.uniform(key_scale, (NPAN,), jnp.float32, 0.0, math.log(10.0 / 3.0)))
    scale = ramp * spread
    entries = jnp.clip(jax.random.normal(key_entry, (NPAN, NRHS), jnp.float32), -4.0, 4.0)
    return scale[:, None] * entries


def levels(key, shape, shards, smallest, largest):
    level = 1.0
    for dim, parts in shards:
        steps = jax.random.uniform(jax.random.fold_in(jax.random.fold_in(key, 6), dim), (parts,), jnp.float32, smallest / len(shards), largest / len(shards))
        level = level * jnp.repeat(jnp.exp(steps), shape[dim] // parts).reshape((-1,) + (1,) * (len(shape) - 1 - dim))
    return level


def gaussian(stream_key, shape, scale, bound, cuts=(), held_as=jnp.bfloat16):
    drawn = jax.random.normal(stream_key, shape, jnp.float32) * scale
    if len(cuts) > 0:
        drawn = levels(stream_key, shape, cuts, -0.22, 0.18) * drawn
    return jnp.clip(drawn, min=-bound, max=bound).astype(held_as)


def setup_inputs(seed: int = 0, part: int = 0) -> dict:
    key_of = jax.random.split(jax.random.key(seed), 9)
    own_keys = jax.random.split(jax.random.fold_in(key_of[8], part), 9)
    rhs = draw_rhs(jax.random.fold_in(jax.random.fold_in(key_of[8], part), 71), part)
    order = draw_order(jax.random.fold_in(key_of[8], 71), part)
    diag = jnp.clip(jnp.exp(math.log(8.0) - 1.3862944 * jax.random.uniform(key_of[2], (NPAN,), jnp.float32) ** levels(key_of[2], (NPAN,), ((0, 128),), -0.2, 0.2)), 2.0, 8.0)
    blocks = gaussian(key_of[3], (NBLK, BLK, BLK), (NEAR_ROW * BLK) ** -0.5, 0.3125, ((0, 128),))
    near_rows = draw_near_rows(jax.random.fold_in(key_of[8], 71), part)
    near_cols = draw_near_cols(jax.random.fold_in(key_of[8], 71), part)
    gen_u = gaussian(key_of[6], (LEVELS, NPAN, K), K ** -0.5, 0.5, ((1, 32), (2, 4)))
    gen_v = gaussian(key_of[7], (LEVELS, NPAN, K), (NPAN // 2) ** -0.5, 0.03125, ((1, 32), (2, 4)))
    return dict(rhs=rhs, order=order, diag=diag, blocks=blocks, near_rows=near_rows, near_cols=near_cols, gen_u=gen_u, gen_v=gen_v)


EPSILON = 1e-06

def operator_apply(vector, diag, blocks, near_rows, near_cols, gen_u, gen_v):
    narrow = vector.astype(jnp.bfloat16)
    wide = narrow.astype(jnp.float32)
    far = jnp.zeros((NPAN, NRHS), jnp.float32)
    for level in range(LEVELS):
        node_size = PAN_LEAF * 2 ** level
        nodes = NPAN // node_size
        v_part = gen_v[level].astype(jnp.float32).reshape(nodes, node_size, K)
        x_part = wide.reshape(nodes, node_size, NRHS)
        sums = jnp.einsum('msk,msn->mkn', v_part, x_part, precision=lax.Precision.HIGHEST)
        sums = sums.astype(jnp.bfloat16)
        swapped = sums.reshape(nodes // 2, 2, K, NRHS)[:, ::-1].reshape(nodes, K, NRHS)
        u_part = gen_u[level].astype(jnp.float32).reshape(nodes, node_size, K)
        term = jnp.einsum('msk,mkn->msn', u_part, swapped.astype(jnp.float32), precision=lax.Precision.HIGHEST)
        far = far + term.reshape(NPAN, NRHS)
    per_group = NEAR_ROW * PAN_DEV // BLK
    groups = NBLK // per_group
    column_view = narrow.reshape(NPAN // BLK, BLK, NRHS)

    def add_group(carry, item):
        values, rows, cols = item
        picked = column_view[cols].astype(jnp.float32)
        product = jnp.einsum('kij,kjn->kin', values.astype(jnp.float32), picked, precision=lax.Precision.HIGHEST)
        return (carry.at[rows].add(product), None)
    near_init = jnp.zeros((NPAN // BLK, BLK, NRHS), jnp.float32)
    near, unused = lax.scan(add_group, near_init, (blocks.reshape(groups, per_group, BLK, BLK), near_rows.reshape(groups, per_group).astype(jnp.int32), near_cols.reshape(groups, per_group).astype(jnp.int32)))
    return diag[:, None] * vector + near.reshape(NPAN, NRHS) + far

def reference(rhs, order, diag, blocks, near_rows, near_cols, gen_u, gen_v):

    def apply(vector):
        return operator_apply(vector, diag, blocks, near_rows, near_cols, gen_u, gen_v)
    start = rhs[order]
    beta = jnp.sqrt(lax.optimization_barrier(jnp.sum(start * start, axis=0)) + EPSILON)
    basis_one = start / beta
    image_one = apply(basis_one)
    h11 = lax.optimization_barrier(jnp.sum(basis_one * image_one, axis=0))
    rest_one = image_one - h11 * basis_one
    h21 = jnp.sqrt(lax.optimization_barrier(jnp.sum(rest_one * rest_one, axis=0)) + EPSILON)
    basis_two = rest_one / h21
    image_two = apply(basis_two)
    h12 = lax.optimization_barrier(jnp.sum(basis_one * image_two, axis=0))
    h22 = lax.optimization_barrier(jnp.sum(basis_two * image_two, axis=0))
    rest_two = image_two - h12 * basis_one - h22 * basis_two
    h32 = jnp.sqrt(lax.optimization_barrier(jnp.sum(rest_two * rest_two, axis=0)) + EPSILON)
    r_one = jnp.sqrt(h11 * h11 + h21 * h21)
    cos_one = h11 / r_one
    sin_one = h21 / r_one
    top = cos_one * h12 + sin_one * h22
    low = cos_one * h22 - sin_one * h12
    r_two = jnp.sqrt(low * low + h32 * h32)
    y_two = low / r_two * (-sin_one * beta) / r_two
    y_one = (cos_one * beta - top * y_two) / r_one
    tree_solution = y_one * basis_one + y_two * basis_two
    tree_residual = (beta - y_one * h11 - y_two * h12) * basis_one - (y_one * h21 + y_two * h22) * basis_two - y_two * rest_two
    solution = jnp.zeros_like(rhs).at[order].set(tree_solution)
    residual = jnp.zeros_like(rhs).at[order].set(tree_residual)
    return (solution, residual)
```

```python
import functools

import jax
import jax.numpy as jnp
from jax import lax
from jax.experimental import pallas as pl
from jax.experimental.pallas import tpu as pltpu
from jax.sharding import PartitionSpec as P

EPSILON = 1e-06
MESH = pl.DeviceIdType.MESH
F32, BF16 = jnp.float32, jnp.bfloat16
BLK = 128
KEEP = 128
PLANE = [(dy, dx) for dy in range(4) for dx in range(4)]


def flip(value, bit):
    return value + bit - 2 * bit * lax.rem(lax.div(value, bit), 2)


def dot(a, b, contract=((1,), (0,))):
    return lax.dot_general(a, b, (contract, ((), ())), preferred_element_type=F32)


def kernel(
    order_ref, diag_ref, rows_ref, cols_ref, rhs_hbm, blocks_hbm, gu_hbm, gv_hbm, sol_ref, res_ref,
    s_ref, blk, vt, ut, pt, pm, vp, up, bm, xg, cs, dg, vec, img, img2,
    sb, l1b, l0b, r24, r1, r0, zs, zr, g24, g1, g0, cf24, cf1, cf0, ext0, ext1, ps, pr, pz, pzr,
    lsem, vsem, usem, s1s, s1r, s2s, s2r, s3s, s3r, nes, ner, qs, qr, zqs, zqr,
):
    leaf, y, core = (lax.axis_index(name) for name in ("leaf", "rank", "rhs"))
    x, z = lax.rem(leaf, 4), lax.div(leaf, 4)
    xs = [x, flip(x, 1), flip(x, 2), 3 - x]
    ys = [y] + [lax.rem(y + k, 4) for k in (1, 2, 3)]
    back = [y] + [lax.rem(y + 4 - k, 4) for k in (1, 2, 3)]
    zs_of = [z]
    for bit in (1, 2, 4):
        zs_of = zs_of + [flip(v, bit) for v in zs_of]
    slot = y * 4 + x
    slot1 = y * 2 + lax.rem(x, 2)
    sends = []

    def plane_id(dy, dx):
        return (z * 4 + xs[dx], ys[dy], core)

    def column_id(dz):
        return (zs_of[dz] * 4 + x, y, core)

    def remote(src, dst, send, recv, to):
        return pltpu.make_async_remote_copy(
            src_ref=src, dst_ref=dst, send_sem=send, recv_sem=recv, device_id=to, device_id_type=MESH
        )

    def push(*what):
        copy = remote(*what)
        copy.start()
        sends.append(copy)

    load_s = pltpu.make_async_copy(rhs_hbm, s_ref, lsem.at[0])
    load_b = pltpu.make_async_copy(blocks_hbm, blk, lsem.at[1])
    own_cols = pl.ds(pl.multiple_of(y * 512, 512), 512)
    load_v = pltpu.make_async_copy(gv_hbm.at[:, :, own_cols], vt.at[:, y], lsem.at[2])
    load_u = pltpu.make_async_copy(gu_hbm.at[:, :, own_cols], ut.at[:, y], lsem.at[3])
    for load in (load_s, load_v, load_b, load_u):
        load.start()

    barrier = pltpu.get_barrier_semaphore()
    peers = [plane_id(dy, dx) for dy, dx in PLANE[1:]] + [column_id(dz) for dz in range(1, 8)]
    for peer in peers:
        pl.semaphore_signal(barrier, inc=1, device_id=peer, device_id_type=MESH)

    ol = order_ref[...] - (leaf * 4 + y) * 512
    row = lax.broadcasted_iota(jnp.int32, (512, 512), 0)
    col = lax.broadcasted_iota(jnp.int32, (512, 512), 1)
    hit = row == ol
    dg[...] = jnp.broadcast_to(
        jnp.sum(jnp.where(hit, jnp.broadcast_to(diag_ref[...], (512, 512)), 0.0), axis=1, keepdims=True), (512, 256)
    )
    hot = jnp.where(hit, 1.0, 0.0).astype(BF16)
    for r in range(4):
        pt[r] = hot[:, r * BLK : (r + 1) * BLK]

    load_s.wait()
    s = s_ref[...]
    sq = s * s
    zero = jnp.zeros((1, 256), F32)

    def sum_start(i, values):
        ps[i] = jnp.concatenate(values + [zero] * (8 - len(values)), 0)
        for d, (dy, dx) in enumerate(PLANE):
            if d:
                push(ps.at[i], pr.at[i, d], qs.at[i, d], qr.at[i, d], plane_id(dy, dx))

    def sum_turn(i):
        total = ps[i]
        for d, (dy, dx) in enumerate(PLANE):
            if d:
                remote(ps.at[i], pr.at[i, d], qs.at[i, d], qr.at[i, d], plane_id(dy, dx)).wait_recv()
                total = total + pr[i, d]
        pz[i] = total
        for dz in range(1, 8):
            push(pz.at[i], pzr.at[i, dz], zqs.at[i, dz], zqr.at[i, dz], column_id(dz))

    def sum_end(i):
        total = pz[i]
        for dz in range(1, 8):
            remote(pz.at[i], pzr.at[i, dz], zqs.at[i, dz], zqr.at[i, dz], column_id(dz)).wait_recv()
            total = total + pzr[i, dz]
        return total

    def column_sum(value):
        return jnp.sum(value, axis=0, keepdims=True)

    first = [column_sum(sq), column_sum(dg[...] * sq)]
    pl.semaphore_wait(barrier, len(peers))

    def spread(gen, held, sems):
        for dy in (1, 3, 2):
            columns = pl.ds(pl.multiple_of(ys[dy] * 512, 512), 512)
            push(gen.at[:, :, columns], held.at[:, y], sems.at[0, dy], sems.at[1, dy], plane_id(dy, 0))

    def gathered(gen, held, sems):
        for dy in (1, 3, 2):
            remote(
                gen.at[:, :, pl.ds(0, 512)], held.at[:, back[dy]], sems.at[0, dy], sems.at[1, dy], plane_id(dy, 0)
            ).wait_recv()

    sum_start(0, first)
    spread(gv_hbm, vt, vsem)
    spread(gu_hbm, ut, usem)

    eye = jnp.where(row == col, 1.0, 0.0).astype(BF16)
    pm[...] = dot(eye, hot, ((1,), (1,))).astype(BF16)
    load_b.wait()
    for k in range(12):
        at = jnp.clip(rows_ref[k] - (leaf * 4 + y) * 4, 0, 3)
        bm[:, k * BLK : (k + 1) * BLK] = dot(pt[at], blk[k]).astype(BF16)
    sum_turn(0)
    load_v.wait()
    gathered(gv_hbm, vt, vsem)
    vp[...] = dot(vt[...].reshape(640, 512), pm[...]).astype(BF16)

    totals = sum_end(0)
    s_sum, d_sum = totals[0:1], totals[1:2]
    beta = jnp.sqrt(s_sum + EPSILON)
    inv_beta = 1.0 / beta
    shift = d_sum / (beta * beta)
    b1b1 = s_sum / (beta * beta)

    def apply_start(a, q, q_low=None):
        ext = (ext0, ext1)[a]
        ct = dot(vp[...], q)
        if q_low is not None:
            ct = ct + dot(vp[...], q_low)
        ct = ct.astype(BF16)
        for t in range(16):
            g, c = t // 2, t % 2
            for b in range(3):
                sb[a, t, b * 16 : b * 16 + 16] = ct[(b + 2) * KEEP + g * 16 :, c * 128 :][:16, :128]
        for d, (dy, dx) in enumerate(PLANE):
            if d:
                push(sb.at[a, ys[dy] * 4 + xs[dx]], r24.at[a, d], s1s.at[a, d], s1r.at[a, d], plane_id(dy, dx))
        for t in range(4):
            for c in range(2):
                l0b[a, t, c * 32 : c * 32 + 32] = ct[t * 32 :, c * 128 :][:32, :128]
        for dy in range(4):
            n = 16 + dy
            push(l0b.at[a, ys[dy]], r0.at[a, dy], s1s.at[a, n], s1r.at[a, n], plane_id(dy, 1))
        for t in range(8):
            for c in range(2):
                l1b[a, t, c * 16 : c * 16 + 16] = ct[KEEP + t * 16 :, c * 128 :][:16, :128]
        for dy in range(4):
            for dx in (2, 3):
                n, k = 20 + dy * 2 + dx - 2, dy * 2 + dx - 2
                there = ys[dy] * 2 + lax.rem(xs[dx], 2)
                push(l1b.at[a, there], r1.at[a, k], s1s.at[a, n], s1r.at[a, n], plane_id(dy, dx))
        ext[4:8] = dot(pm[...], q).astype(BF16).reshape(4, BLK, 256)
        push(ext.at[pl.ds(4, 4)], ext.at[pl.ds(0, 4)], nes.at[a, 0], ner.at[a, 0], plane_id(1, 0))
        push(ext.at[pl.ds(4, 4)], ext.at[pl.ds(8, 4)], nes.at[a, 1], ner.at[a, 1], plane_id(3, 0))

    def apply_end(a, out, before=None):
        ext = (ext0, ext1)[a]
        total = sb[a, slot].astype(F32)
        for d, (dy, dx) in enumerate(PLANE):
            if d:
                remote(sb.at[a, 0], r24.at[a, d], s1s.at[a, d], s1r.at[a, d], plane_id(dy, dx)).wait_recv()
                total = total + r24[a, d].astype(F32)
        zs[a] = total
        for dz in range(1, 8):
            b = 0 if dz < 2 else 1 if dz < 4 else 2
            push(zs.at[a, pl.ds(b * 16, 16)], zr.at[a, dz], s2s.at[a, dz], s2r.at[a, dz], column_id(dz))
        total = jnp.zeros((64, 128), F32)
        for dy in range(4):
            n = 16 + dy
            remote(l0b.at[a, 0], r0.at[a, dy], s1s.at[a, n], s1r.at[a, n], plane_id(dy, 1)).wait_recv()
            total = total + r0[a, dy].astype(F32)
        g0[a] = total.astype(BF16)
        cf0[a, y] = g0[a]
        for dy in range(1, 4):
            n = 16 + dy
            push(g0.at[a], cf0.at[a, y], s3s.at[a, n], s3r.at[a, n], plane_id(dy, 0))
        total = jnp.zeros((32, 128), F32)
        for dy in range(4):
            for dx in (2, 3):
                n, k = 20 + dy * 2 + dx - 2, dy * 2 + dx - 2
                remote(l1b.at[a, 0], r1.at[a, k], s1s.at[a, n], s1r.at[a, n], plane_id(dy, dx)).wait_recv()
                total = total + r1[a, k].astype(F32)
        g1[a] = total.astype(BF16)
        cf1[a, slot1] = g1[a]
        for dy in range(4):
            for dx in range(2):
                if dy or dx:
                    n = 20 + dy * 2 + dx
                    push(g1.at[a], cf1.at[a, slot1], s3s.at[a, n], s3r.at[a, n], plane_id(dy, dx))
        parts = []
        for b, group in enumerate(((1,), (2, 3), (4, 5, 6, 7))):
            total = jnp.zeros((16, 128), F32)
            for dz in group:
                remote(
                    zs.at[a, pl.ds(b * 16, 16)], zr.at[a, dz], s2s.at[a, dz], s2r.at[a, dz], column_id(dz)
                ).wait_recv()
                total = total + zr[a, dz]
            g24[a, b * 16 : b * 16 + 16] = total.astype(BF16)
        cf24[a, slot] = g24[a]
        for d, (dy, dx) in enumerate(PLANE):
            if d:
                push(g24.at[a], cf24.at[a, slot], s3s.at[a, d], s3r.at[a, d], plane_id(dy, dx))

        if before is not None:
            before()
        remote(
            ext.at[pl.ds(4, 4)], ext.at[pl.ds(0, 4)], nes.at[a, 0], ner.at[a, 0], plane_id(1, 0)
        ).wait_recv()
        remote(
            ext.at[pl.ds(4, 4)], ext.at[pl.ds(8, 4)], nes.at[a, 1], ner.at[a, 1], plane_id(3, 0)
        ).wait_recv()
        for k in range(12):
            at = jnp.clip(cols_ref[k] - (leaf * 4 + y) * 4 + 4, 0, 11)
            xg[k * BLK : (k + 1) * BLK] = ext[at]
        out[...] = dot(bm[...], xg[...])

        for dy in range(1, 4):
            n = 16 + dy
            remote(g0.at[a], cf0.at[a, back[dy]], s3s.at[a, n], s3r.at[a, n], plane_id(dy, 0)).wait_recv()
        for t in range(4):
            for c in range(2):
                cs[t * 32 : t * 32 + 32, c * 128 : c * 128 + 128] = cf0[a, t, c * 32 : c * 32 + 32]
        for dy in range(4):
            for dx in range(2):
                if dy or dx:
                    n = 20 + dy * 2 + dx
                    there = back[dy] * 2 + lax.rem(xs[dx], 2)
                    remote(g1.at[a], cf1.at[a, there], s3s.at[a, n], s3r.at[a, n], plane_id(dy, dx)).wait_recv()
        for t in range(8):
            for c in range(2):
                cs[KEEP + t * 16 : KEEP + t * 16 + 16, c * 128 : c * 128 + 128] = cf1[a, t, c * 16 : c * 16 + 16]
        out[...] += dot(up[:, : 2 * KEEP], cs[: 2 * KEEP])
        for d, (dy, dx) in enumerate(PLANE):
            if d:
                there = back[dy] * 4 + xs[dx]
                remote(g24.at[a], cf24.at[a, there], s3s.at[a, d], s3r.at[a, d], plane_id(dy, dx)).wait_recv()
        for t in range(16):
            g, c = t // 2, t % 2
            for b in range(3):
                at = (b + 2) * KEEP + g * 16
                cs[at : at + 16, c * 128 : c * 128 + 128] = cf24[a, t, b * 16 : b * 16 + 16]
        out[...] += dot(up[:, 2 * KEEP :], cs[2 * KEEP :])

    b1 = s * inv_beta
    apply_start(0, b1.astype(BF16))

    def own_u():
        load_u.wait()
        gathered(gu_hbm, ut, usem)
        hot_t = jnp.concatenate([pt[r] for r in range(4)], 1)
        up[...] = dot(hot_t, ut[...].reshape(640, 512), ((1,), (1,))).astype(BF16)

    apply_end(0, img, own_u)
    b1 = s_ref[...] * inv_beta
    p = (dg[...] - shift) * b1 + img[...]
    vec[...] = p
    q = p.astype(BF16)
    apply_start(1, q, (p - q.astype(F32)).astype(BF16))
    apply_end(1, img2)
    b1 = s_ref[...] * inv_beta
    p = vec[...]
    w = dg[...] * p + img2[...]
    img2[...] = w
    sum_start(1, [column_sum(v) for v in (b1 * p, p * p, b1 * w, p * w, w * w)])
    sum_turn(1)
    totals = sum_end(1)
    e, pp, f, g, ww = (totals[k : k + 1] for k in range(5))
    h11 = e + shift * b1b1
    delta = h11 - shift
    h21 = jnp.sqrt(jnp.maximum(pp - 2.0 * delta * e + delta * delta * b1b1, 0.0) + EPSILON)
    h12 = (f - delta * h11) / h21
    h22 = (g - delta * (pp + shift * e) - delta * f + delta * delta * h11) / (h21 * h21)
    of_w = 1.0 / h21
    of_p = -(delta + h22) / h21
    of_b = -(delta * shift / h21 + h12 - h22 * delta / h21)
    rest = (
        of_w * of_w * ww + of_p * of_p * pp + of_b * of_b * b1b1
        + 2.0 * (of_w * of_p * g + of_w * of_b * f + of_p * of_b * e)
    )
    h32 = jnp.sqrt(jnp.maximum(rest, 0.0) + EPSILON)
    r_one = jnp.sqrt(h11 * h11 + h21 * h21)
    cos_one = h11 / r_one
    sin_one = h21 / r_one
    top = cos_one * h12 + sin_one * h22
    low = cos_one * h22 - sin_one * h12
    r_two = jnp.sqrt(low * low + h32 * h32)
    y_two = low / r_two * (-sin_one * beta) / r_two
    y_one = (cos_one * beta - top * y_two) / r_one
    of_one = beta - y_one * h11 - y_two * h12
    of_two = -(y_one * h21 + y_two * h22)
    sol_ref[...] = (y_one - y_two * delta / h21) * b1 + (y_two / h21) * p
    res_ref[...] = (
        (of_one - of_two * delta / h21 - y_two * of_b) * b1
        + (of_two / h21 - y_two * of_p) * p
        - (y_two * of_w) * w
    )
    for copy in sends:
        copy.wait_send()


def local(rhs, order, diag, blocks, near_rows, near_cols, gen_u, gen_v):
    vmem, smem, hbm = (pl.BlockSpec(memory_space=m) for m in (pltpu.VMEM, pltpu.SMEM, pltpu.HBM))
    scratch = [
        ((512, 256), F32),
        ((12, BLK, BLK), BF16),
        ((5, 4, 32, 512), BF16),
        ((5, 4, 32, 512), BF16),
        ((4, 512, BLK), BF16),
        ((512, 512), BF16),
        ((640, 512), BF16),
        ((512, 640), BF16),
        ((512, 1536), BF16),
        ((1536, 256), BF16),
        ((640, 256), BF16),
        ((512, 256), F32),
        ((512, 256), F32),
        ((512, 256), F32),
        ((512, 256), F32),
        ((2, 16, 48, 128), BF16),
        ((2, 8, 32, 128), BF16),
        ((2, 4, 64, 128), BF16),
        ((2, 16, 48, 128), BF16),
        ((2, 8, 32, 128), BF16),
        ((2, 4, 64, 128), BF16),
        ((2, 48, 128), F32),
        ((2, 8, 16, 128), F32),
        ((2, 48, 128), BF16),
        ((2, 32, 128), BF16),
        ((2, 64, 128), BF16),
        ((2, 16, 48, 128), BF16),
        ((2, 8, 32, 128), BF16),
        ((2, 4, 64, 128), BF16),
        ((12, BLK, 256), BF16),
        ((12, BLK, 256), BF16),
        ((2, 8, 256), F32),
        ((2, 16, 8, 256), F32),
        ((2, 8, 256), F32),
        ((2, 8, 8, 256), F32),
    ]
    sems = [(4,), (2, 4), (2, 4), (2, 28), (2, 28), (2, 8), (2, 8), (2, 28), (2, 28), (2, 2), (2, 2), (2, 16), (2, 16), (2, 8), (2, 8)]
    return pl.pallas_call(
        kernel,
        out_shape=[jax.ShapeDtypeStruct(rhs.shape, F32)] * 2,
        in_specs=[vmem, vmem, smem, smem, hbm, hbm, hbm, hbm],
        out_specs=[vmem, vmem],
        scratch_shapes=[pltpu.VMEM(*s) for s in scratch] + [pltpu.SemaphoreType.DMA(s) for s in sems],
        compiler_params=pltpu.CompilerParams(
            collective_id=0, has_side_effects=True, vmem_limit_bytes=60 * 1024 * 1024
        ),
    )(
        order.reshape(1, -1), diag.reshape(1, -1), near_rows, near_cols, rhs, blocks,
        gen_u.transpose(0, 2, 1), gen_v.transpose(0, 2, 1),
    )


def solution(mesh):
    in_specs = (
        P(("leaf", "rank"), "rhs"),
        P(("leaf", "rank")),
        P(("leaf", "rank")),
        P(("leaf", "rank"), None, None),
        P(("leaf", "rank")),
        P(("leaf", "rank")),
        P(None, "leaf", "rank"),
        P(None, "leaf", "rank"),
    )
    out_specs = (P(("leaf", "rank"), "rhs"), P(("leaf", "rank"), "rhs"))
    return jax.shard_map(local, mesh=mesh, in_specs=in_specs, out_specs=out_specs, check_vma=False)
```

```python
import functools

import jax
import jax.numpy as jnp
from jax import lax
from jax.experimental import pallas as pl
from jax.experimental.pallas import tpu as pltpu
from jax.sharding import PartitionSpec as P

EPSILON = 1e-06
MESH = pl.DeviceIdType.MESH
F32, BF16 = jnp.float32, jnp.bfloat16
BLK = 128
KEEP = 128
ROOM, LAST = 40_000_000, 8_000_000
PLANE = [(dy, dx) for dy in range(4) for dx in range(4)]


def flip(value, bit):
    return value + bit - 2 * bit * lax.rem(lax.div(value, bit), 2)


def dot(a, b, contract=((1,), (0,))):
    return lax.dot_general(a, b, (contract, ((), ())), preferred_element_type=F32)


def kernel(
    order_hbm, diag_hbm, rows_hbm, cols_hbm, rhs_hbm, blocks_hbm, gu_hbm, gv_hbm, vec, img2, c0, c1, c2, c3, c4,
    order_ref, diag_ref, rows_ref, cols_ref, s_ref, blk, vt, ut, pt, pm, vp, up, bm, xg, cs, dg, img,
    sb, l1b, l0b, r24, r1, r0, zs, zr, g24, g1, g0, cf24, cf1, cf0, ext0, ext1, ps, pr, pz, pzr,
    lsem, vsem, usem, vfsem, ufsem, s1s, s1r, s2s, s2r, s3s, s3r, nes, ner, qs, qr, zqs, zqr,
):
    leaf, y, core = (lax.axis_index(name) for name in ("leaf", "rank", "rhs"))
    x, z = lax.rem(leaf, 4), lax.div(leaf, 4)
    xs = [x, flip(x, 1), flip(x, 2), 3 - x]
    ys = [y] + [lax.rem(y + k, 4) for k in (1, 2, 3)]
    back = [y] + [lax.rem(y + 4 - k, 4) for k in (1, 2, 3)]
    zs_of = [z]
    for bit in (1, 2, 4):
        zs_of = zs_of + [flip(v, bit) for v in zs_of]
    slot = y * 4 + x
    slot1 = y * 2 + lax.rem(x, 2)
    twin = (leaf, y, 1 - core)
    sends = []

    def plane_id(dy, dx):
        return (z * 4 + xs[dx], ys[dy], core)

    def column_id(dz):
        return (zs_of[dz] * 4 + x, y, core)

    def remote(src, dst, send, recv, to):
        return pltpu.make_async_remote_copy(
            src_ref=src, dst_ref=dst, send_sem=send, recv_sem=recv, device_id=to, device_id_type=MESH
        )

    def push(*what):
        copy = remote(*what)
        copy.start()
        sends.append(copy)

    barrier = pltpu.get_barrier_semaphore()
    peers = [plane_id(dy, dx) for dy, dx in PLANE[1:]] + [column_id(dz) for dz in range(1, 8)] + [twin]
    for peer in peers:
        pl.semaphore_signal(barrier, inc=1, device_id=peer, device_id_type=MESH)

    own_cols = pl.ds(pl.multiple_of(y * 512, 512), 512)
    pairs = (
        (order_hbm, order_ref), (diag_hbm, diag_ref), (rhs_hbm, s_ref), (rows_hbm, rows_ref), (cols_hbm, cols_ref),
        (blocks_hbm, blk), (gv_hbm.at[:, :, :, own_cols], vt.at[:, y]), (gu_hbm.at[:, :, :, own_cols], ut.at[:, y]),
    )
    loads = [pltpu.make_async_copy(src, dst, lsem.at[k]) for k, (src, dst) in enumerate(pairs)]
    for load in loads:
        load.start()
    load_o, load_d, load_s, load_r, load_c, load_b, load_v, load_u = loads

    load_o.wait()
    load_d.wait()
    ol = order_ref[...] - (leaf * 4 + y) * 512
    row = lax.broadcasted_iota(jnp.int32, (512, 512), 0)
    col = lax.broadcasted_iota(jnp.int32, (512, 512), 1)
    hit = row == ol
    dg[...] = jnp.broadcast_to(
        jnp.sum(jnp.where(hit, jnp.broadcast_to(diag_ref[...], (512, 512)), 0.0), axis=1, keepdims=True), (512, 256)
    )
    hot = jnp.where(hit, 1.0, 0.0).astype(BF16)
    for r in range(4):
        pt[r] = hot[:, r * BLK : (r + 1) * BLK]

    load_s.wait()
    s = s_ref[...]
    sq = s * s

    def sum_start(i, values):
        rows = [v[:, c * 128 : c * 128 + 128] for v in values for c in range(2)]
        ps[i, : len(rows)] = jnp.concatenate(rows, 0)
        for d, (dy, dx) in enumerate(PLANE):
            if d:
                part = pl.ds(0, 8 * (1 + i))
                push(ps.at[i, part], pr.at[i, d, part], qs.at[i, d], qr.at[i, d], plane_id(dy, dx))

    def sum_turn(i):
        part = pl.ds(0, 8 * (1 + i))
        total = ps[i, part]
        for d, (dy, dx) in enumerate(PLANE):
            if d:
                remote(ps.at[i, part], pr.at[i, d, part], qs.at[i, d], qr.at[i, d], plane_id(dy, dx)).wait_recv()
                total = total + pr[i, d, part]
        pz[i, part] = total
        for dz in range(1, 8):
            push(pz.at[i, part], pzr.at[i, dz, part], zqs.at[i, dz], zqr.at[i, dz], column_id(dz))

    def sum_end(i, count):
        part = pl.ds(0, 8 * (1 + i))
        total = pz[i, part]
        for dz in range(1, 8):
            remote(pz.at[i, part], pzr.at[i, dz, part], zqs.at[i, dz], zqr.at[i, dz], column_id(dz)).wait_recv()
            total = total + pzr[i, dz, part]
        return [jnp.concatenate([total[2 * k : 2 * k + 1], total[2 * k + 1 : 2 * k + 2]], 1) for k in range(count)]

    def column_sum(value):
        return jnp.sum(value, axis=0, keepdims=True)

    ps[...] = jnp.zeros_like(ps)
    first = [column_sum(sq), column_sum(dg[...] * sq)]
    pl.semaphore_wait(barrier, len(peers))

    def spread(gen, held, sems):
        for dy in (1, 3, 2):
            columns = pl.ds(pl.multiple_of(ys[dy] * 512, 512), 512)
            push(
                gen.at[:, core, :, columns], held.at[:, y, core], sems.at[0, dy], sems.at[1, dy], plane_id(dy, 0)
            )

    def hand_on(gen, held, sems, on):
        for dy in (1, 3, 2):
            mine = held.at[:, back[dy], core]
            remote(
                gen.at[:, core, :, pl.ds(0, 512)], mine, sems.at[0, dy], sems.at[1, dy], plane_id(dy, 0)
            ).wait_recv()
            push(mine, mine, on.at[0, dy], on.at[1, dy], twin)

    def gathered(held, on):
        for dy in (1, 3, 2):
            mine, other = held.at[:, back[dy], core], held.at[:, back[dy], 1 - core]
            remote(mine, other, on.at[0, dy], on.at[1, dy], twin).wait_recv()

    sum_start(0, first)
    spread(gv_hbm, vt, vsem)

    eye = jnp.where(row == col, 1.0, 0.0).astype(BF16)
    pm[...] = dot(eye, hot, ((1,), (1,))).astype(BF16)
    load_b.wait()
    load_r.wait()
    load_c.wait()
    for k in range(12):
        at = jnp.clip(rows_ref[k] - (leaf * 4 + y) * 4, 0, 3)
        bm[:, k * BLK : (k + 1) * BLK] = dot(pt[at], blk[k]).astype(BF16)
    sum_turn(0)
    load_v.wait()
    hand_on(gv_hbm, vt, vsem, vfsem)
    spread(gu_hbm, ut, usem)
    gathered(vt, vfsem)
    hot = jnp.concatenate([pt[r] for r in range(4)], 1)
    vp[...] = dot(vt[...].reshape(640, 512), hot, ((1,), (1,))).astype(BF16)

    s_sum, d_sum = sum_end(0, 2)
    beta = jnp.sqrt(s_sum + EPSILON)
    inv_beta = 1.0 / beta
    shift = d_sum / (beta * beta)
    b1b1 = s_sum / (beta * beta)

    def apply_start(a, q):
        ext = (ext0, ext1)[a]
        ct = dot(vp[...], q).astype(BF16)
        for t in range(16):
            g, c = t // 2, t % 2
            for b in range(3):
                sb[a, t, b * 16 : b * 16 + 16] = ct[(b + 2) * KEEP + g * 16 :, c * 128 :][:16, :128]
        for d, (dy, dx) in enumerate(PLANE):
            if d:
                push(sb.at[a, ys[dy] * 4 + xs[dx]], r24.at[a, d], s1s.at[a, d], s1r.at[a, d], plane_id(dy, dx))
        for t in range(4):
            for c in range(2):
                l0b[a, t, c * 32 : c * 32 + 32] = ct[t * 32 :, c * 128 :][:32, :128]
        for dy in range(4):
            n = 16 + dy
            push(l0b.at[a, ys[dy]], r0.at[a, dy], s1s.at[a, n], s1r.at[a, n], plane_id(dy, 1))
        for t in range(8):
            for c in range(2):
                l1b[a, t, c * 16 : c * 16 + 16] = ct[KEEP + t * 16 :, c * 128 :][:16, :128]
        for dy in range(4):
            for dx in (2, 3):
                n, k = 20 + dy * 2 + dx - 2, dy * 2 + dx - 2
                there = ys[dy] * 2 + lax.rem(xs[dx], 2)
                push(l1b.at[a, there], r1.at[a, k], s1s.at[a, n], s1r.at[a, n], plane_id(dy, dx))
        ext[4:8] = dot(pm[...], q).astype(BF16).reshape(4, BLK, 256)
        push(ext.at[pl.ds(4, 4)], ext.at[pl.ds(0, 4)], nes.at[a, 0], ner.at[a, 0], plane_id(1, 0))
        push(ext.at[pl.ds(4, 4)], ext.at[pl.ds(8, 4)], nes.at[a, 1], ner.at[a, 1], plane_id(3, 0))

    def apply_end(a, out, early=None, before=None):
        ext = (ext0, ext1)[a]
        total = sb[a, slot].astype(F32)
        for d, (dy, dx) in enumerate(PLANE):
            if d:
                remote(sb.at[a, 0], r24.at[a, d], s1s.at[a, d], s1r.at[a, d], plane_id(dy, dx)).wait_recv()
                total = total + r24[a, d].astype(F32)
        zs[a] = total
        for dz in range(1, 8):
            b = 0 if dz < 2 else 1 if dz < 4 else 2
            push(zs.at[a, pl.ds(b * 16, 16)], zr.at[a, dz], s2s.at[a, dz], s2r.at[a, dz], column_id(dz))
        if early is not None:
            early()
        total = jnp.zeros((64, 128), F32)
        for dy in range(4):
            n = 16 + dy
            remote(l0b.at[a, 0], r0.at[a, dy], s1s.at[a, n], s1r.at[a, n], plane_id(dy, 1)).wait_recv()
            total = total + r0[a, dy].astype(F32)
        g0[a] = total.astype(BF16)
        cf0[a, y] = g0[a]
        for dy in range(1, 4):
            n = 16 + dy
            push(g0.at[a], cf0.at[a, y], s3s.at[a, n], s3r.at[a, n], plane_id(dy, 0))
        total = jnp.zeros((32, 128), F32)
        for dy in range(4):
            for dx in (2, 3):
                n, k = 20 + dy * 2 + dx - 2, dy * 2 + dx - 2
                remote(l1b.at[a, 0], r1.at[a, k], s1s.at[a, n], s1r.at[a, n], plane_id(dy, dx)).wait_recv()
                total = total + r1[a, k].astype(F32)
        g1[a] = total.astype(BF16)
        cf1[a, slot1] = g1[a]
        for dy in range(4):
            for dx in range(2):
                if dy or dx:
                    n = 20 + dy * 2 + dx
                    push(g1.at[a], cf1.at[a, slot1], s3s.at[a, n], s3r.at[a, n], plane_id(dy, dx))
        parts = []
        for b, group in enumerate(((1,), (2, 3), (4, 5, 6, 7))):
            total = jnp.zeros((16, 128), F32)
            for dz in group:
                remote(
                    zs.at[a, pl.ds(b * 16, 16)], zr.at[a, dz], s2s.at[a, dz], s2r.at[a, dz], column_id(dz)
                ).wait_recv()
                total = total + zr[a, dz]
            g24[a, b * 16 : b * 16 + 16] = total.astype(BF16)
        cf24[a, slot] = g24[a]
        for d, (dy, dx) in enumerate(PLANE):
            if d:
                push(g24.at[a], cf24.at[a, slot], s3s.at[a, d], s3r.at[a, d], plane_id(dy, dx))

        if before is not None:
            before()
        remote(
            ext.at[pl.ds(4, 4)], ext.at[pl.ds(0, 4)], nes.at[a, 0], ner.at[a, 0], plane_id(1, 0)
        ).wait_recv()
        remote(
            ext.at[pl.ds(4, 4)], ext.at[pl.ds(8, 4)], nes.at[a, 1], ner.at[a, 1], plane_id(3, 0)
        ).wait_recv()
        for k in range(12):
            at = jnp.clip(cols_ref[k] - (leaf * 4 + y) * 4 + 4, 0, 11)
            xg[k * BLK : (k + 1) * BLK] = ext[at]
        out[...] = dot(bm[...], xg[...])

        for dy in range(1, 4):
            n = 16 + dy
            remote(g0.at[a], cf0.at[a, back[dy]], s3s.at[a, n], s3r.at[a, n], plane_id(dy, 0)).wait_recv()
        for t in range(4):
            for c in range(2):
                cs[t * 32 : t * 32 + 32, c * 128 : c * 128 + 128] = cf0[a, t, c * 32 : c * 32 + 32]
        for dy in range(4):
            for dx in range(2):
                if dy or dx:
                    n = 20 + dy * 2 + dx
                    there = back[dy] * 2 + lax.rem(xs[dx], 2)
                    remote(g1.at[a], cf1.at[a, there], s3s.at[a, n], s3r.at[a, n], plane_id(dy, dx)).wait_recv()
        for t in range(8):
            for c in range(2):
                cs[KEEP + t * 16 : KEEP + t * 16 + 16, c * 128 : c * 128 + 128] = cf1[a, t, c * 16 : c * 16 + 16]
        out[...] += dot(up[:, : 2 * KEEP], cs[: 2 * KEEP])
        for d, (dy, dx) in enumerate(PLANE):
            if d:
                there = back[dy] * 4 + xs[dx]
                remote(g24.at[a], cf24.at[a, there], s3s.at[a, d], s3r.at[a, d], plane_id(dy, dx)).wait_recv()
        for t in range(16):
            g, c = t // 2, t % 2
            for b in range(3):
                at = (b + 2) * KEEP + g * 16
                cs[at : at + 16, c * 128 : c * 128 + 128] = cf24[a, t, b * 16 : b * 16 + 16]
        out[...] += dot(up[:, 2 * KEEP :], cs[2 * KEEP :])

    b1 = s * inv_beta
    apply_start(0, b1.astype(BF16))

    def own_u():
        load_u.wait()
        gathered(ut, ufsem)
        hot_t = jnp.concatenate([pt[r] for r in range(4)], 1)
        up[...] = dot(hot_t, ut[...].reshape(640, 512), ((1,), (1,))).astype(BF16)

    apply_end(0, img, lambda: hand_on(gu_hbm, ut, usem, ufsem), own_u)
    b1 = s_ref[...] * inv_beta
    p = (dg[...] - shift) * b1 + img[...]
    vec[...] = p
    apply_start(1, p.astype(BF16))
    apply_end(1, img2)
    b1 = s_ref[...] * inv_beta
    p = vec[...]
    w = dg[...] * p + img2[...]
    img2[...] = w
    sum_start(1, [column_sum(v) for v in (b1 * p, p * p, b1 * w, p * w, w * w)])
    sum_turn(1)
    e, pp, f, g, ww = sum_end(1, 5)
    h11 = e + shift * b1b1
    delta = h11 - shift
    h21 = jnp.sqrt(jnp.maximum(pp - 2.0 * delta * e + delta * delta * b1b1, 0.0) + EPSILON)
    h12 = (f - delta * h11) / h21
    h22 = (g - delta * (pp + shift * e) - delta * f + delta * delta * h11) / (h21 * h21)
    of_w = 1.0 / h21
    of_p = -(delta + h22) / h21
    of_b = -(delta * shift / h21 + h12 - h22 * delta / h21)
    rest = (
        of_w * of_w * ww + of_p * of_p * pp + of_b * of_b * b1b1
        + 2.0 * (of_w * of_p * g + of_w * of_b * f + of_p * of_b * e)
    )
    h32 = jnp.sqrt(jnp.maximum(rest, 0.0) + EPSILON)
    r_one = jnp.sqrt(h11 * h11 + h21 * h21)
    cos_one = h11 / r_one
    sin_one = h21 / r_one
    top = cos_one * h12 + sin_one * h22
    low = cos_one * h22 - sin_one * h12
    r_two = jnp.sqrt(low * low + h32 * h32)
    y_two = low / r_two * (-sin_one * beta) / r_two
    y_one = (cos_one * beta - top * y_two) / r_one
    of_one = beta - y_one * h11 - y_two * h12
    of_two = -(y_one * h21 + y_two * h22)
    rows = (
        (y_one - y_two * delta / h21) * inv_beta,
        y_two / h21,
        (of_one - of_two * delta / h21 - y_two * of_b) * inv_beta,
        of_two / h21 - y_two * of_p,
        -(y_two * of_w),
    )
    for ref, value in zip((c0, c1, c2, c3, c4), rows):
        ref[...] = value
    for copy in sends:
        copy.wait_send()


def combine(rhs, vec, image, c0, c1, c2, c3, c4, sol_hbm, res_hbm, sol, res, sem):
    copies = []
    for k in range(4):
        part = pl.ds(k * 128, 128)
        r, v, m = rhs[part], vec[part], image[part]
        sol[part] = c0[...] * r + c1[...] * v
        copies.append(pltpu.make_async_copy(sol.at[part], sol_hbm.at[part], sem.at[0, k]))
        copies[-1].start()
        res[part] = c2[...] * r + c3[...] * v + c4[...] * m
        copies.append(pltpu.make_async_copy(res.at[part], res_hbm.at[part], sem.at[1, k]))
        copies[-1].start()
    for copy in copies:
        copy.wait()


def local(rhs, order, diag, blocks, near_rows, near_cols, gen_u, gen_v):
    vmem, hbm = (pl.BlockSpec(memory_space=m) for m in (pltpu.VMEM, pltpu.HBM))
    scratch = [
        ((512, 256), F32),
        ((12, BLK, BLK), BF16),
        ((5, 4, 2, 16, 512), BF16),
        ((5, 4, 2, 16, 512), BF16),
        ((4, 512, BLK), BF16),
        ((512, 512), BF16),
        ((640, 512), BF16),
        ((512, 640), BF16),
        ((512, 1536), BF16),
        ((1536, 256), BF16),
        ((640, 256), BF16),
        ((512, 256), F32),
        ((512, 256), F32),
        ((2, 16, 48, 128), BF16),
        ((2, 8, 32, 128), BF16),
        ((2, 4, 64, 128), BF16),
        ((2, 16, 48, 128), BF16),
        ((2, 8, 32, 128), BF16),
        ((2, 4, 64, 128), BF16),
        ((2, 48, 128), F32),
        ((2, 8, 16, 128), F32),
        ((2, 48, 128), BF16),
        ((2, 32, 128), BF16),
        ((2, 64, 128), BF16),
        ((2, 16, 48, 128), BF16),
        ((2, 8, 32, 128), BF16),
        ((2, 4, 64, 128), BF16),
        ((12, BLK, 256), BF16),
        ((12, BLK, 256), BF16),
        ((2, 16, 128), F32),
        ((2, 16, 16, 128), F32),
        ((2, 16, 128), F32),
        ((2, 8, 16, 128), F32),
    ]
    sems = [(8,), (2, 4), (2, 4), (2, 4), (2, 4), (2, 28), (2, 28), (2, 8), (2, 8), (2, 28), (2, 28), (2, 2), (2, 2), (2, 16), (2, 16), (2, 8), (2, 8)]
    vec, image, *coef = pl.pallas_call(
        kernel,
        out_shape=[jax.ShapeDtypeStruct(shape, F32) for shape in (rhs.shape,) * 2 + ((1, 256),) * 5],
        in_specs=[hbm] * 8,
        out_specs=[vmem] * 7,
        scratch_shapes=[pltpu.VMEM((1, 512), jnp.int32), pltpu.VMEM((1, 512), F32)]
        + [pltpu.SMEM((12,), jnp.int32)] * 2
        + [pltpu.VMEM(*s) for s in scratch] + [pltpu.SemaphoreType.DMA(s) for s in sems],
        compiler_params=pltpu.CompilerParams(
            collective_id=0, has_side_effects=True, vmem_limit_bytes=ROOM
        ),
    )(
        *(
            pltpu.with_memory_space_constraint(value, pltpu.HBM)
            for value in (
                order.reshape(1, -1), diag.reshape(1, -1), near_rows, near_cols, rhs, blocks,
                gen_u.transpose(0, 2, 1).reshape(5, 2, 16, -1), gen_v.transpose(0, 2, 1).reshape(5, 2, 16, -1),
            )
        )
    )
    return pl.pallas_call(
        combine,
        out_shape=[jax.ShapeDtypeStruct(rhs.shape, F32)] * 2,
        in_specs=[vmem] * 8,
        out_specs=[hbm] * 2,
        scratch_shapes=[pltpu.VMEM((512, 256), F32)] * 2 + [pltpu.SemaphoreType.DMA((2, 4))],
        compiler_params=pltpu.CompilerParams(vmem_limit_bytes=LAST),
    )(rhs, vec, image, *coef)


def solution(mesh):
    in_specs = (
        P(("leaf", "rank"), "rhs"),
        P(("leaf", "rank")),
        P(("leaf", "rank")),
        P(("leaf", "rank"), None, None),
        P(("leaf", "rank")),
        P(("leaf", "rank")),
        P(None, "leaf", "rank"),
        P(None, "leaf", "rank"),
    )
    out_specs = (P(("leaf", "rank"), "rhs"), P(("leaf", "rank"), "rhs"))
    return jax.shard_map(local, mesh=mesh, in_specs=in_specs, out_specs=out_specs, check_vma=False)
```

```python
import functools

import jax
import jax.numpy as jnp
from jax import lax
from jax.experimental import pallas as pl
from jax.experimental.pallas import tpu as pltpu
from jax.sharding import PartitionSpec as P

EPSILON = 1e-06
MESH = pl.DeviceIdType.MESH
F32, BF16 = jnp.float32, jnp.bfloat16
BLK = 128
KEEP = 128
ROOM, LAST = 40_000_000, 8_000_000
HOPS = (0, 1, 2, 1)
PLANE = [(dy, dx) for dy in range(4) for dx in range(4)]
FAR = sorted(range(1, 16), key=lambda d: -HOPS[d // 4] - HOPS[d % 4])
FAR_Z = (4, 5, 7, 3, 6, 2, 1)


def flip(value, bit):
    return value + bit - 2 * bit * lax.rem(lax.div(value, bit), 2)


def dot(a, b, contract=((1,), (0,))):
    return lax.dot_general(a, b, (contract, ((), ())), preferred_element_type=F32)


def kernel(
    order_hbm, diag_hbm, rows_hbm, cols_hbm, rhs_hbm, blocks_hbm, gu_hbm, gv_hbm, vec, img2, c0, c1, c2, c3, c4,
    order_ref, diag_ref, rows_ref, cols_ref, s_ref, blk, vt, ut, pt, pm, vp, up, bm, xg, cs, dg, img,
    sb4, sb, l1b, l0b, r4, r24, r1, r0, zs, zr, g4, g24, g1, g0, cf4, cf24, cf1, cf0, ext0, ext1, ps, pr, pz, pzr,
    lsem, vsem, usem, vfsem, ufsem, s1s, s1r, s2s, s2r, s3s, s3r, s4s, s4r, s5s, s5r, nes, ner, qs, qr, zqs, zqr,
):
    leaf, y, core = (lax.axis_index(name) for name in ("leaf", "rank", "rhs"))
    x, z = lax.rem(leaf, 4), lax.div(leaf, 4)
    xs = [x, flip(x, 1), flip(x, 2), 3 - x]
    ys = [y] + [lax.rem(y + k, 4) for k in (1, 2, 3)]
    back = [y] + [lax.rem(y + 4 - k, 4) for k in (1, 2, 3)]
    zs_of = [z]
    for bit in (1, 2, 4):
        zs_of = zs_of + [flip(v, bit) for v in zs_of]
    slot = y * 4 + x
    slot1 = y * 2 + lax.rem(x, 2)
    twin = (leaf, y, 1 - core)
    sends = []

    def plane_id(dy, dx):
        return (z * 4 + xs[dx], ys[dy], core)

    def column_id(dz):
        return (zs_of[dz] * 4 + x, y, core)

    def remote(src, dst, send, recv, to):
        return pltpu.make_async_remote_copy(
            src_ref=src, dst_ref=dst, send_sem=send, recv_sem=recv, device_id=to, device_id_type=MESH
        )

    def push(*what):
        copy = remote(*what)
        copy.start()
        sends.append(copy)

    barrier = pltpu.get_barrier_semaphore()
    peers = [plane_id(dy, dx) for dy, dx in PLANE[1:]] + [column_id(dz) for dz in range(1, 8)] + [twin]
    for peer in peers:
        pl.semaphore_signal(barrier, inc=1, device_id=peer, device_id_type=MESH)

    own_cols = pl.ds(pl.multiple_of(y * 512, 512), 512)
    pairs = (
        (order_hbm, order_ref), (diag_hbm, diag_ref), (rhs_hbm, s_ref), (rows_hbm, rows_ref), (cols_hbm, cols_ref),
        (blocks_hbm, blk), (gv_hbm.at[:, :, :, own_cols], vt.at[:, y]), (gu_hbm.at[:, :, :, own_cols], ut.at[:, y]),
    )
    loads = [pltpu.make_async_copy(src, dst, lsem.at[k]) for k, (src, dst) in enumerate(pairs)]
    for load in loads:
        load.start()
    load_o, load_d, load_s, load_r, load_c, load_b, load_v, load_u = loads

    load_o.wait()
    load_d.wait()
    ol = order_ref[...] - (leaf * 4 + y) * 512
    row = lax.broadcasted_iota(jnp.int32, (512, 512), 0)
    col = lax.broadcasted_iota(jnp.int32, (512, 512), 1)
    hit = row == ol
    dg[...] = jnp.broadcast_to(
        jnp.sum(jnp.where(hit, jnp.broadcast_to(diag_ref[...], (512, 512)), 0.0), axis=1, keepdims=True), (512, 256)
    )
    hot = jnp.where(hit, 1.0, 0.0).astype(BF16)
    for r in range(4):
        pt[r] = hot[:, r * BLK : (r + 1) * BLK]

    load_s.wait()
    s = s_ref[...]
    sq = s * s

    def sum_start(i, values):
        rows = [v[:, c * 128 : c * 128 + 128] for v in values for c in range(2)]
        ps[i, : len(rows)] = jnp.concatenate(rows, 0)
        part = pl.ds(0, 8 + 8 * i)
        for d in FAR:
            push(ps.at[i, part], pr.at[i, d, part], qs.at[i, d], qr.at[i, d], plane_id(*PLANE[d]))

    def sum_turn(i):
        part = pl.ds(0, 8 + 8 * i)
        total = ps[i, part]
        for d, (dy, dx) in enumerate(PLANE):
            if d:
                remote(ps.at[i, part], pr.at[i, d, part], qs.at[i, d], qr.at[i, d], plane_id(dy, dx)).wait_recv()
                total = total + pr[i, d, part]
        pz[i, part] = total
        for dz in FAR_Z:
            push(pz.at[i, part], pzr.at[i, dz, part], zqs.at[i, dz], zqr.at[i, dz], column_id(dz))

    def sum_end(i, count):
        part = pl.ds(0, 8 + 8 * i)
        total = pz[i, part]
        for dz in range(1, 8):
            remote(pz.at[i, part], pzr.at[i, dz, part], zqs.at[i, dz], zqr.at[i, dz], column_id(dz)).wait_recv()
            total = total + pzr[i, dz, part]
        return [jnp.concatenate([total[2 * k : 2 * k + 1], total[2 * k + 1 : 2 * k + 2]], 1) for k in range(count)]

    def column_sum(value):
        return jnp.sum(value, axis=0, keepdims=True)

    ps[...] = jnp.zeros_like(ps)
    first = [column_sum(sq), column_sum(dg[...] * sq)]
    pl.semaphore_wait(barrier, len(peers))

    def spread(gen, held, sems):
        for dy in (1, 3, 2):
            columns = pl.ds(pl.multiple_of(ys[dy] * 512, 512), 512)
            push(
                gen.at[:, core, :, columns], held.at[:, y, core], sems.at[0, dy], sems.at[1, dy], plane_id(dy, 0)
            )

    def hand_on(gen, held, sems, on):
        for dy in (1, 3, 2):
            mine = held.at[:, back[dy], core]
            remote(
                gen.at[:, core, :, pl.ds(0, 512)], mine, sems.at[0, dy], sems.at[1, dy], plane_id(dy, 0)
            ).wait_recv()
            push(mine, mine, on.at[0, dy], on.at[1, dy], twin)

    def gathered(held, on):
        for dy in (1, 3, 2):
            mine, other = held.at[:, back[dy], core], held.at[:, back[dy], 1 - core]
            remote(mine, other, on.at[0, dy], on.at[1, dy], twin).wait_recv()

    sum_start(0, first)
    spread(gv_hbm, vt, vsem)

    eye = jnp.where(row == col, 1.0, 0.0).astype(BF16)
    pm[...] = dot(eye, hot, ((1,), (1,))).astype(BF16)
    load_b.wait()
    load_r.wait()
    load_c.wait()
    for k in range(12):
        at = jnp.clip(rows_ref[k] - (leaf * 4 + y) * 4, 0, 3)
        bm[:, k * BLK : (k + 1) * BLK] = dot(pt[at], blk[k]).astype(BF16)
    sum_turn(0)
    load_v.wait()
    hand_on(gv_hbm, vt, vsem, vfsem)
    spread(gu_hbm, ut, usem)
    gathered(vt, vfsem)
    hot = jnp.concatenate([pt[r] for r in range(4)], 1)
    vp[...] = dot(vt[...].reshape(640, 512), hot, ((1,), (1,))).astype(BF16)

    s_sum, d_sum = sum_end(0, 2)
    beta = jnp.sqrt(s_sum + EPSILON)
    inv_beta = 1.0 / beta
    shift = d_sum / (beta * beta)
    b1b1 = s_sum / (beta * beta)

    def apply_start(a, q):
        ext = (ext0, ext1)[a]
        ct = dot(vp[4 * KEEP :], q).astype(BF16)
        for t in range(16):
            g, c = t // 2, t % 2
            sb4[a, t] = ct[g * 16 :, c * 128 :][:16, :128]
        for d in FAR:
            dy, dx = PLANE[d]
            push(sb4.at[a, ys[dy] * 4 + xs[dx]], r4.at[a, d], s4s.at[a, d], s4r.at[a, d], plane_id(dy, dx))
        ct = dot(vp[: 4 * KEEP], q).astype(BF16)
        for t in range(16):
            g, c = t // 2, t % 2
            for b in range(2):
                sb[a, t, b * 16 : b * 16 + 16] = ct[(b + 2) * KEEP + g * 16 :, c * 128 :][:16, :128]
        for d in FAR:
            dy, dx = PLANE[d]
            push(sb.at[a, ys[dy] * 4 + xs[dx]], r24.at[a, d], s1s.at[a, d], s1r.at[a, d], plane_id(dy, dx))
        for t in range(4):
            for c in range(2):
                l0b[a, t, c * 32 : c * 32 + 32] = ct[t * 32 :, c * 128 :][:32, :128]
        for dy in range(4):
            n = 16 + dy
            push(l0b.at[a, ys[dy]], r0.at[a, dy], s1s.at[a, n], s1r.at[a, n], plane_id(dy, 1))
        for t in range(8):
            for c in range(2):
                l1b[a, t, c * 16 : c * 16 + 16] = ct[KEEP + t * 16 :, c * 128 :][:16, :128]
        for dy in range(4):
            for dx in (2, 3):
                n, k = 20 + dy * 2 + dx - 2, dy * 2 + dx - 2
                there = ys[dy] * 2 + lax.rem(xs[dx], 2)
                push(l1b.at[a, there], r1.at[a, k], s1s.at[a, n], s1r.at[a, n], plane_id(dy, dx))
        ext[4:8] = dot(pm[...], q).astype(BF16).reshape(4, BLK, 256)
        push(ext.at[pl.ds(4, 4)], ext.at[pl.ds(0, 4)], nes.at[a, 0], ner.at[a, 0], plane_id(1, 0))
        push(ext.at[pl.ds(4, 4)], ext.at[pl.ds(8, 4)], nes.at[a, 1], ner.at[a, 1], plane_id(3, 0))

    def apply_end(a, out, early=None, before=None):
        ext = (ext0, ext1)[a]
        total = sb4[a, slot].astype(F32)
        for d, (dy, dx) in enumerate(PLANE):
            if d:
                remote(sb4.at[a, 0], r4.at[a, d], s4s.at[a, d], s4r.at[a, d], plane_id(dy, dx)).wait_recv()
                total = total + r4[a, d].astype(F32)
        zs[a, 32:48] = total

        def push_z(dz):
            b = 0 if dz < 2 else 1 if dz < 4 else 2
            push(zs.at[a, pl.ds(b * 16, 16)], zr.at[a, dz], s2s.at[a, dz], s2r.at[a, dz], column_id(dz))

        for dz in (4, 5, 7, 6):
            push_z(dz)
        total = sb[a, slot].astype(F32)
        for d, (dy, dx) in enumerate(PLANE):
            if d:
                remote(sb.at[a, 0], r24.at[a, d], s1s.at[a, d], s1r.at[a, d], plane_id(dy, dx)).wait_recv()
                total = total + r24[a, d].astype(F32)
        zs[a, 0:32] = total
        for dz in (3, 2, 1):
            push_z(dz)
        if early is not None:
            early()
        total = jnp.zeros((64, 128), F32)
        for dy in range(4):
            n = 16 + dy
            remote(l0b.at[a, 0], r0.at[a, dy], s1s.at[a, n], s1r.at[a, n], plane_id(dy, 1)).wait_recv()
            total = total + r0[a, dy].astype(F32)
        g0[a] = total.astype(BF16)
        cf0[a, y] = g0[a]
        for dy in range(1, 4):
            n = 16 + dy
            push(g0.at[a], cf0.at[a, y], s3s.at[a, n], s3r.at[a, n], plane_id(dy, 0))
        total = jnp.zeros((32, 128), F32)
        for dy in range(4):
            for dx in (2, 3):
                n, k = 20 + dy * 2 + dx - 2, dy * 2 + dx - 2
                remote(l1b.at[a, 0], r1.at[a, k], s1s.at[a, n], s1r.at[a, n], plane_id(dy, dx)).wait_recv()
                total = total + r1[a, k].astype(F32)
        g1[a] = total.astype(BF16)
        cf1[a, slot1] = g1[a]
        for dy in range(4):
            for dx in range(2):
                if dy or dx:
                    n = 20 + dy * 2 + dx
                    push(g1.at[a], cf1.at[a, slot1], s3s.at[a, n], s3r.at[a, n], plane_id(dy, dx))
        def sibling(b, group):
            total = jnp.zeros((16, 128), F32)
            for dz in group:
                remote(
                    zs.at[a, pl.ds(b * 16, 16)], zr.at[a, dz], s2s.at[a, dz], s2r.at[a, dz], column_id(dz)
                ).wait_recv()
                total = total + zr[a, dz]
            return total.astype(BF16)

        g4[a] = sibling(2, (6, 7, 5, 4))
        for d in FAR:
            push(g4.at[a], cf4.at[a, slot], s5s.at[a, d], s5r.at[a, d], plane_id(*PLANE[d]))
        g24[a, 0:16] = sibling(0, (1,))
        g24[a, 16:32] = sibling(1, (2, 3))
        for d in FAR:
            push(g24.at[a], cf24.at[a, slot], s3s.at[a, d], s3r.at[a, d], plane_id(*PLANE[d]))
        cf4[a, slot] = g4[a]
        cf24[a, slot] = g24[a]

        if before is not None:
            before()
        remote(
            ext.at[pl.ds(4, 4)], ext.at[pl.ds(0, 4)], nes.at[a, 0], ner.at[a, 0], plane_id(1, 0)
        ).wait_recv()
        remote(
            ext.at[pl.ds(4, 4)], ext.at[pl.ds(8, 4)], nes.at[a, 1], ner.at[a, 1], plane_id(3, 0)
        ).wait_recv()
        for k in range(12):
            at = jnp.clip(cols_ref[k] - (leaf * 4 + y) * 4 + 4, 0, 11)
            xg[k * BLK : (k + 1) * BLK] = ext[at]
        out[...] = dot(bm[...], xg[...])

        for dy in range(1, 4):
            n = 16 + dy
            remote(g0.at[a], cf0.at[a, back[dy]], s3s.at[a, n], s3r.at[a, n], plane_id(dy, 0)).wait_recv()
        for t in range(4):
            for c in range(2):
                cs[t * 32 : t * 32 + 32, c * 128 : c * 128 + 128] = cf0[a, t, c * 32 : c * 32 + 32]
        for dy in range(4):
            for dx in range(2):
                if dy or dx:
                    n = 20 + dy * 2 + dx
                    there = back[dy] * 2 + lax.rem(xs[dx], 2)
                    remote(g1.at[a], cf1.at[a, there], s3s.at[a, n], s3r.at[a, n], plane_id(dy, dx)).wait_recv()
        for t in range(8):
            for c in range(2):
                cs[KEEP + t * 16 : KEEP + t * 16 + 16, c * 128 : c * 128 + 128] = cf1[a, t, c * 16 : c * 16 + 16]
        out[...] += dot(up[:, : 2 * KEEP], cs[: 2 * KEEP])
        for d, (dy, dx) in enumerate(PLANE):
            if d:
                there = back[dy] * 4 + xs[dx]
                remote(g4.at[a], cf4.at[a, there], s5s.at[a, d], s5r.at[a, d], plane_id(dy, dx)).wait_recv()
        for t in range(16):
            g, c = t // 2, t % 2
            at = 4 * KEEP + g * 16
            cs[at : at + 16, c * 128 : c * 128 + 128] = cf4[a, t]
        for d, (dy, dx) in enumerate(PLANE):
            if d:
                there = back[dy] * 4 + xs[dx]
                remote(g24.at[a], cf24.at[a, there], s3s.at[a, d], s3r.at[a, d], plane_id(dy, dx)).wait_recv()
        for t in range(16):
            g, c = t // 2, t % 2
            for b in range(2):
                at = (b + 2) * KEEP + g * 16
                cs[at : at + 16, c * 128 : c * 128 + 128] = cf24[a, t, b * 16 : b * 16 + 16]
        out[...] += dot(up[:, 2 * KEEP :], cs[2 * KEEP :])

    b1 = s * inv_beta
    apply_start(0, b1.astype(BF16))

    def own_u():
        load_u.wait()
        gathered(ut, ufsem)
        hot_t = jnp.concatenate([pt[r] for r in range(4)], 1)
        up[...] = dot(hot_t, ut[...].reshape(640, 512), ((1,), (1,))).astype(BF16)

    apply_end(0, img, lambda: hand_on(gu_hbm, ut, usem, ufsem), own_u)
    b1 = s_ref[...] * inv_beta
    p = (dg[...] - shift) * b1 + img[...]
    vec[...] = p
    apply_start(1, p.astype(BF16))
    apply_end(1, img2)
    b1 = s_ref[...] * inv_beta
    p = vec[...]
    w = dg[...] * p + img2[...]
    sum_start(1, [column_sum(v) for v in (b1 * p, p * p, b1 * w, p * w, w * w)])
    img2[...] = w
    done = len(sends)
    for copy in sends:
        copy.wait_send()
    sum_turn(1)
    e, pp, f, g, ww = sum_end(1, 5)
    h11 = e + shift * b1b1
    delta = h11 - shift
    h21 = jnp.sqrt(jnp.maximum(pp - 2.0 * delta * e + delta * delta * b1b1, 0.0) + EPSILON)
    h12 = (f - delta * h11) / h21
    h22 = (g - delta * (pp + shift * e) - delta * f + delta * delta * h11) / (h21 * h21)
    of_w = 1.0 / h21
    of_p = -(delta + h22) / h21
    of_b = -(delta * shift / h21 + h12 - h22 * delta / h21)
    rest = (
        of_w * of_w * ww + of_p * of_p * pp + of_b * of_b * b1b1
        + 2.0 * (of_w * of_p * g + of_w * of_b * f + of_p * of_b * e)
    )
    h32 = jnp.sqrt(jnp.maximum(rest, 0.0) + EPSILON)
    r_one = jnp.sqrt(h11 * h11 + h21 * h21)
    cos_one = h11 / r_one
    sin_one = h21 / r_one
    top = cos_one * h12 + sin_one * h22
    low = cos_one * h22 - sin_one * h12
    r_two = jnp.sqrt(low * low + h32 * h32)
    y_two = low / r_two * (-sin_one * beta) / r_two
    y_one = (cos_one * beta - top * y_two) / r_one
    of_one = beta - y_one * h11 - y_two * h12
    of_two = -(y_one * h21 + y_two * h22)
    rows = (
        (y_one - y_two * delta / h21) * inv_beta,
        y_two / h21,
        (of_one - of_two * delta / h21 - y_two * of_b) * inv_beta,
        of_two / h21 - y_two * of_p,
        -(y_two * of_w),
    )
    for ref, value in zip((c0, c1, c2, c3, c4), rows):
        ref[...] = value
    for copy in sends[done:]:
        copy.wait_send()


def combine(rhs, vec, image, c0, c1, c2, c3, c4, sol_hbm, res_hbm, sol, res, sem):
    copies = []
    for k in range(4):
        part = pl.ds(k * 128, 128)
        r, v, m = rhs[part], vec[part], image[part]
        sol[part] = c0[...] * r + c1[...] * v
        copies.append(pltpu.make_async_copy(sol.at[part], sol_hbm.at[part], sem.at[0, k]))
        copies[-1].start()
        res[part] = c2[...] * r + c3[...] * v + c4[...] * m
        copies.append(pltpu.make_async_copy(res.at[part], res_hbm.at[part], sem.at[1, k]))
        copies[-1].start()
    for copy in copies:
        copy.wait()


def local(rhs, order, diag, blocks, near_rows, near_cols, gen_u, gen_v):
    vmem, hbm = (pl.BlockSpec(memory_space=m) for m in (pltpu.VMEM, pltpu.HBM))
    scratch = [
        ((512, 256), F32),
        ((12, BLK, BLK), BF16),
        ((5, 4, 2, 16, 512), BF16),
        ((5, 4, 2, 16, 512), BF16),
        ((4, 512, BLK), BF16),
        ((512, 512), BF16),
        ((640, 512), BF16),
        ((512, 640), BF16),
        ((512, 1536), BF16),
        ((1536, 256), BF16),
        ((640, 256), BF16),
        ((512, 256), F32),
        ((512, 256), F32),
        ((2, 16, 16, 128), BF16),
        ((2, 16, 32, 128), BF16),
        ((2, 8, 32, 128), BF16),
        ((2, 4, 64, 128), BF16),
        ((2, 16, 16, 128), BF16),
        ((2, 16, 32, 128), BF16),
        ((2, 8, 32, 128), BF16),
        ((2, 4, 64, 128), BF16),
        ((2, 48, 128), F32),
        ((2, 8, 16, 128), F32),
        ((2, 16, 128), BF16),
        ((2, 32, 128), BF16),
        ((2, 32, 128), BF16),
        ((2, 64, 128), BF16),
        ((2, 16, 16, 128), BF16),
        ((2, 16, 32, 128), BF16),
        ((2, 8, 32, 128), BF16),
        ((2, 4, 64, 128), BF16),
        ((12, BLK, 256), BF16),
        ((12, BLK, 256), BF16),
        ((2, 16, 128), F32),
        ((2, 16, 16, 128), F32),
        ((2, 16, 128), F32),
        ((2, 8, 16, 128), F32),
    ]
    sems = [(8,), (2, 4), (2, 4), (2, 4), (2, 4)]
    sems += [(2, 28), (2, 28), (2, 8), (2, 8), (2, 28), (2, 28), (2, 16), (2, 16), (2, 16), (2, 16)]
    sems += [(2, 2), (2, 2), (2, 16), (2, 16), (2, 8), (2, 8)]
    vec, image, *coef = pl.pallas_call(
        kernel,
        out_shape=[jax.ShapeDtypeStruct(shape, F32) for shape in (rhs.shape,) * 2 + ((1, 256),) * 5],
        in_specs=[hbm] * 8,
        out_specs=[vmem] * 7,
        scratch_shapes=[pltpu.VMEM((1, 512), jnp.int32), pltpu.VMEM((1, 512), F32)]
        + [pltpu.SMEM((12,), jnp.int32)] * 2
        + [pltpu.VMEM(*s) for s in scratch] + [pltpu.SemaphoreType.DMA(s) for s in sems],
        compiler_params=pltpu.CompilerParams(
            collective_id=0, has_side_effects=True, vmem_limit_bytes=ROOM
        ),
    )(
        *(
            pltpu.with_memory_space_constraint(value, pltpu.HBM)
            for value in (
                order.reshape(1, -1), diag.reshape(1, -1), near_rows, near_cols, rhs, blocks,
                gen_u.transpose(0, 2, 1).reshape(5, 2, 16, -1), gen_v.transpose(0, 2, 1).reshape(5, 2, 16, -1),
            )
        )
    )
    return pl.pallas_call(
        combine,
        out_shape=[jax.ShapeDtypeStruct(rhs.shape, F32)] * 2,
        in_specs=[vmem] * 8,
        out_specs=[hbm] * 2,
        scratch_shapes=[pltpu.VMEM((512, 256), F32)] * 2 + [pltpu.SemaphoreType.DMA((2, 4))],
        compiler_params=pltpu.CompilerParams(vmem_limit_bytes=LAST),
    )(rhs, vec, image, *coef)


def solution(mesh):
    in_specs = (
        P(("leaf", "rank"), "rhs"),
        P(("leaf", "rank")),
        P(("leaf", "rank")),
        P(("leaf", "rank"), None, None),
        P(("leaf", "rank")),
        P(("leaf", "rank")),
        P(None, "leaf", "rank"),
        P(None, "leaf", "rank"),
    )
    out_specs = (P(("leaf", "rank"), "rhs"), P(("leaf", "rank"), "rhs"))
    return jax.shard_map(local, mesh=mesh, in_specs=in_specs, out_specs=out_specs, check_vma=False)
```

```python
import functools

import jax
import jax.numpy as jnp
from jax import lax
from jax.experimental import pallas as pl
from jax.experimental.pallas import tpu as pltpu
from jax.sharding import PartitionSpec as P

EPSILON = 1e-06
MESH = pl.DeviceIdType.MESH
F32, BF16 = jnp.float32, jnp.bfloat16
BLK = 128
KEEP = 128
ROOM, LAST = 40_000_000, 8_000_000
HOPS = (0, 1, 2, 1)
PLANE = [(dy, dx) for dy in range(4) for dx in range(4)]
FAR = sorted(range(1, 16), key=lambda d: -HOPS[d // 4] - HOPS[d % 4])
FAR_Z = (4, 5, 7, 3, 6, 2, 1)


def flip(value, bit):
    return value + bit - 2 * bit * lax.rem(lax.div(value, bit), 2)


def dot(a, b, contract=((1,), (0,))):
    return lax.dot_general(a, b, (contract, ((), ())), preferred_element_type=F32)


def kernel(
    order_hbm, diag_hbm, rows_hbm, cols_hbm, rhs_hbm, blocks_hbm, gu_hbm, gv_hbm, vec, img2, c0, c1, c2, c3, c4,
    order_ref, diag_ref, rows_ref, cols_ref, s_ref, blk, vt, ut, pt, pm, vp, up, bm, xg, cs, dg, img,
    sb4, sb, l1b, l0b, r4, r24, r1, r0, zs, zr, g4, g24, g1, g0, cf4, cf24, cf1, cf0, ext0, ext1, ps, pr, pz, pzr,
    sem,
):
    leaf, y, core = (lax.axis_index(name) for name in ("leaf", "rank", "rhs"))
    x, z = lax.rem(leaf, 4), lax.div(leaf, 4)
    xs = [x, flip(x, 1), flip(x, 2), 3 - x]
    ys = [y] + [lax.rem(y + k, 4) for k in (1, 2, 3)]
    back = [y] + [lax.rem(y + 4 - k, 4) for k in (1, 2, 3)]
    zs_of = [z]
    for bit in (1, 2, 4):
        zs_of = zs_of + [flip(v, bit) for v in zs_of]
    slot = y * 4 + x
    slot1 = y * 2 + lax.rem(x, 2)
    twin = (leaf, y, 1 - core)
    sends = []

    def plane_id(dy, dx):
        return (z * 4 + xs[dx], ys[dy], core)

    def column_id(dz):
        return (zs_of[dz] * 4 + x, y, core)

    def remote(src, dst, send, recv, to):
        return pltpu.make_async_remote_copy(
            src_ref=src, dst_ref=dst, send_sem=send, recv_sem=recv, device_id=to, device_id_type=MESH
        )

    def push(*what):
        remote(*what).start()

    taken = []

    def fresh(count):
        first = len(taken)
        taken.extend(range(count))
        return [sem.at[first + k] for k in range(count)]

    def drain(ref, done):
        pltpu.make_async_copy(ref, ref, done).wait()

    barrier = pltpu.get_barrier_semaphore()
    peers = [plane_id(dy, dx) for dy, dx in PLANE[1:]] + [column_id(dz) for dz in range(1, 8)] + [twin]
    for peer in peers:
        pl.semaphore_signal(barrier, inc=1, device_id=peer, device_id_type=MESH)

    own_cols = pl.ds(pl.multiple_of(y * 512, 512), 512)
    pairs = (
        (order_hbm, order_ref), (diag_hbm, diag_ref), (rhs_hbm, s_ref), (rows_hbm, rows_ref), (cols_hbm, cols_ref),
        (blocks_hbm, blk), (gv_hbm.at[:, :, :, own_cols], vt.at[:, y]), (gu_hbm.at[:, :, :, own_cols], ut.at[:, y]),
    )
    loads = [pltpu.make_async_copy(src, dst, done) for (src, dst), done in zip(pairs, fresh(8))]
    for load in loads:
        load.start()
    load_o, load_d, load_s, load_r, load_c, load_b, load_v, load_u = loads

    load_o.wait()
    load_d.wait()
    ol = order_ref[...] - (leaf * 4 + y) * 512
    row = lax.broadcasted_iota(jnp.int32, (512, 512), 0)
    col = lax.broadcasted_iota(jnp.int32, (512, 512), 1)
    hit = row == ol
    dg[...] = jnp.broadcast_to(
        jnp.sum(jnp.where(hit, jnp.broadcast_to(diag_ref[...], (512, 512)), 0.0), axis=1, keepdims=True), (512, 256)
    )
    hot = jnp.where(hit, 1.0, 0.0).astype(BF16)
    for r in range(4):
        pt[r] = hot[:, r * BLK : (r + 1) * BLK]

    load_s.wait()
    s = s_ref[...]
    sq = s * s

    sum_sems = [fresh(4), fresh(4)]

    def sum_start(i, values):
        rows = [v[:, c * 128 : c * 128 + 128] for v in values for c in range(2)]
        ps[i, : len(rows)] = jnp.concatenate(rows, 0)
        part, (sent, got, _, _) = pl.ds(0, 8 + 8 * i), sum_sems[i]
        for d in FAR:
            push(ps.at[i, part], pr.at[i, d, part], sent, got, plane_id(*PLANE[d]))
        sends.append((pr.at[i, pl.ds(1, 15), part], sent))

    def sum_turn(i):
        part, (_, got, sent, _) = pl.ds(0, 8 + 8 * i), sum_sems[i]
        drain(pr.at[i, pl.ds(1, 15), part], got)
        total = ps[i, part]
        for d in range(1, 16):
            total = total + pr[i, d, part]
        pz[i, part] = total
        for dz in FAR_Z:
            push(pz.at[i, part], pzr.at[i, dz, part], sent, sum_sems[i][3], column_id(dz))
        sends.append((pzr.at[i, pl.ds(1, 7), part], sent))

    def sum_end(i, count):
        part = pl.ds(0, 8 + 8 * i)
        drain(pzr.at[i, pl.ds(1, 7), part], sum_sems[i][3])
        total = pz[i, part]
        for dz in range(1, 8):
            total = total + pzr[i, dz, part]
        return [total[2 * k : 2 * k + 2] for k in range(count)]

    def wide(value):
        return jnp.concatenate([value[0:1], value[1:2]], 1)

    def column_sum(value):
        return jnp.sum(value, axis=0, keepdims=True)

    ps[...] = jnp.zeros_like(ps)
    first = [column_sum(sq), column_sum(dg[...] * sq)]
    pl.semaphore_wait(barrier, len(peers))

    v_sems, u_sems = fresh(6), fresh(6)

    def spread(gen, held, sems):
        for k, dy in enumerate((1, 3, 2)):
            columns = pl.ds(pl.multiple_of(ys[dy] * 512, 512), 512)
            push(gen.at[:, core, :, columns], held.at[:, y, core], sems[3], sems[k], plane_id(dy, 0))
        sends.append((held.at[:, pl.ds(0, 3), core], sems[3]))

    def hand_on(gen, held, sems):
        for k, dy in enumerate((1, 3, 2)):
            mine = held.at[:, back[dy], core]
            drain(mine, sems[k])
            push(mine, mine, sems[4], sems[5], twin)
        sends.append((held.at[:, pl.ds(0, 3), core], sems[4]))

    def gathered(held, sems):
        drain(held.at[:, pl.ds(0, 3), 1 - core], sems[5])

    sum_start(0, first)
    spread(gv_hbm, vt, v_sems)

    eye = jnp.where(row == col, 1.0, 0.0).astype(BF16)
    pm[...] = dot(eye, hot, ((1,), (1,))).astype(BF16)
    load_b.wait()
    load_r.wait()
    load_c.wait()
    for k in range(12):
        at = jnp.clip(rows_ref[k] - (leaf * 4 + y) * 4, 0, 3)
        bm[:, k * BLK : (k + 1) * BLK] = dot(pt[at], blk[k]).astype(BF16)
    sum_turn(0)
    hand_on(gv_hbm, vt, v_sems)
    spread(gu_hbm, ut, u_sems)
    load_v.wait()
    gathered(vt, v_sems)
    vp[...] = dot(vt[...].reshape(640, 512), hot, ((1,), (1,))).astype(BF16)

    s_sum, d_sum = sum_end(0, 2)
    beta = jnp.sqrt(s_sum + EPSILON)
    inv_beta = 1.0 / beta
    inv_wide = wide(inv_beta)
    shift = d_sum / (beta * beta)
    b1b1 = s_sum / (beta * beta)

    stage_sems = [[fresh(2) for _ in range(11)] for _ in range(2)]

    def apply_start(a, q):
        four, pair, zero, one, _, _, _, _, _, _, near = stage_sems[a]
        ext = (ext0, ext1)[a]
        ct = dot(vp[4 * KEEP :], q).astype(BF16)
        for t in range(16):
            g, c = t // 2, t % 2
            sb4[a, t] = ct[g * 16 :, c * 128 :][:16, :128]
        for d in FAR:
            dy, dx = PLANE[d]
            push(sb4.at[a, ys[dy] * 4 + xs[dx]], r4.at[a, d], *four, plane_id(dy, dx))
        sends.append((r4.at[a, pl.ds(1, 15)], four[0]))
        ct = dot(vp[: 4 * KEEP], q).astype(BF16)
        for t in range(16):
            g, c = t // 2, t % 2
            for b in range(2):
                sb[a, t, b * 16 : b * 16 + 16] = ct[(b + 2) * KEEP + g * 16 :, c * 128 :][:16, :128]
        for d in FAR:
            dy, dx = PLANE[d]
            push(sb.at[a, ys[dy] * 4 + xs[dx]], r24.at[a, d], *pair, plane_id(dy, dx))
        sends.append((r24.at[a, pl.ds(1, 15)], pair[0]))
        for t in range(4):
            for c in range(2):
                l0b[a, t, c * 32 : c * 32 + 32] = ct[t * 32 :, c * 128 :][:32, :128]
        for dy in range(4):
            push(l0b.at[a, ys[dy]], r0.at[a, dy], *zero, plane_id(dy, 1))
        sends.append((r0.at[a], zero[0]))
        for t in range(8):
            for c in range(2):
                l1b[a, t, c * 16 : c * 16 + 16] = ct[KEEP + t * 16 :, c * 128 :][:16, :128]
        for dy in range(4):
            for dx in (2, 3):
                there = ys[dy] * 2 + lax.rem(xs[dx], 2)
                push(l1b.at[a, there], r1.at[a, dy * 2 + dx - 2], *one, plane_id(dy, dx))
        sends.append((r1.at[a], one[0]))
        ext[4:8] = dot(pm[...], q).astype(BF16).reshape(4, BLK, 256)
        push(ext.at[pl.ds(4, 4)], ext.at[pl.ds(0, 4)], *near, plane_id(1, 0))
        push(ext.at[pl.ds(4, 4)], ext.at[pl.ds(8, 4)], *near, plane_id(3, 0))
        sends.append((ext.at[pl.ds(0, 8)], near[0]))

    def apply_end(a, out, before=None):
        ext = (ext0, ext1)[a]
        four, pair, zero, one, z_four, z_pair, all_four, all_pair, all_zero, all_one, near = stage_sems[a]

        def push_z(dz, pair_of):
            b = 0 if dz < 2 else 1 if dz < 4 else 2
            push(zs.at[a, pl.ds(b * 16, 16)], zr.at[a, dz], *pair_of, column_id(dz))

        drain(r4.at[a, pl.ds(1, 15)], four[1])
        total = sb4[a, slot].astype(F32)
        for d in range(1, 16):
            total = total + r4[a, d].astype(F32)
        zs[a, 32:48] = total
        for dz in (4, 5, 7, 6):
            push_z(dz, z_four)
        drain(r24.at[a, pl.ds(1, 15)], pair[1])
        total = sb[a, slot].astype(F32)
        for d in range(1, 16):
            total = total + r24[a, d].astype(F32)
        zs[a, 0:32] = total
        for dz in (3, 2, 1):
            push_z(dz, z_pair)
        sends.append((zr.at[a, pl.ds(4, 4)], z_four[0]))
        sends.append((zr.at[a, pl.ds(1, 3)], z_pair[0]))

        drain(r0.at[a], zero[1])
        total = jnp.zeros((64, 128), F32)
        for dy in range(4):
            total = total + r0[a, dy].astype(F32)
        g0[a] = total.astype(BF16)
        for dy in (2, 1, 3):
            push(g0.at[a], cf0.at[a, y], *all_zero, plane_id(dy, 0))
        cf0[a, y] = g0[a]
        sends.append((cf0.at[a, pl.ds(0, 3)], all_zero[0]))
        drain(r1.at[a], one[1])
        total = jnp.zeros((32, 128), F32)
        for k in range(8):
            total = total + r1[a, k].astype(F32)
        g1[a] = total.astype(BF16)
        for dy in (2, 1, 3, 0):
            for dx in (1, 0):
                if dy or dx:
                    push(g1.at[a], cf1.at[a, slot1], *all_one, plane_id(dy, dx))
        cf1[a, slot1] = g1[a]
        sends.append((cf1.at[a, pl.ds(0, 7)], all_one[0]))

        drain(zr.at[a, pl.ds(4, 4)], z_four[1])
        g4[a] = (zr[a, 4] + zr[a, 5] + zr[a, 6] + zr[a, 7]).astype(BF16)
        for d in FAR:
            push(g4.at[a], cf4.at[a, slot], *all_four, plane_id(*PLANE[d]))
        sends.append((cf4.at[a, pl.ds(0, 15)], all_four[0]))
        drain(zr.at[a, pl.ds(1, 3)], z_pair[1])
        g24[a, 0:16] = zr[a, 1].astype(BF16)
        g24[a, 16:32] = (zr[a, 2] + zr[a, 3]).astype(BF16)
        for d in FAR:
            push(g24.at[a], cf24.at[a, slot], *all_pair, plane_id(*PLANE[d]))
        sends.append((cf24.at[a, pl.ds(0, 15)], all_pair[0]))
        cf4[a, slot] = g4[a]
        cf24[a, slot] = g24[a]

        if before is not None:
            before()
        drain(ext.at[pl.ds(0, 8)], near[1])
        for k in range(12):
            at = jnp.clip(cols_ref[k] - (leaf * 4 + y) * 4 + 4, 0, 11)
            xg[k * BLK : (k + 1) * BLK] = ext[at]
        out[...] = dot(bm[...], xg[...])

        drain(cf0.at[a, pl.ds(0, 3)], all_zero[1])
        for t in range(4):
            for c in range(2):
                cs[t * 32 : t * 32 + 32, c * 128 : c * 128 + 128] = cf0[a, t, c * 32 : c * 32 + 32]
        drain(cf1.at[a, pl.ds(0, 7)], all_one[1])
        for t in range(8):
            for c in range(2):
                cs[KEEP + t * 16 : KEEP + t * 16 + 16, c * 128 : c * 128 + 128] = cf1[a, t, c * 16 : c * 16 + 16]
        out[...] += dot(up[:, : 2 * KEEP], cs[: 2 * KEEP])
        drain(cf4.at[a, pl.ds(0, 15)], all_four[1])
        for t in range(16):
            g, c = t // 2, t % 2
            at = 4 * KEEP + g * 16
            cs[at : at + 16, c * 128 : c * 128 + 128] = cf4[a, t]
        out[...] += dot(up[:, 4 * KEEP :], cs[4 * KEEP :])
        drain(cf24.at[a, pl.ds(0, 15)], all_pair[1])
        for t in range(16):
            g, c = t // 2, t % 2
            for b in range(2):
                at = (b + 2) * KEEP + g * 16
                cs[at : at + 16, c * 128 : c * 128 + 128] = cf24[a, t, b * 16 : b * 16 + 16]
        out[...] += dot(up[:, 2 * KEEP : 4 * KEEP], cs[2 * KEEP : 4 * KEEP])

    b1 = s * inv_wide
    apply_start(0, b1.astype(BF16))

    def own_u():
        load_u.wait()
        hand_on(gu_hbm, ut, u_sems)
        gathered(ut, u_sems)
        hot_t = jnp.concatenate([pt[r] for r in range(4)], 1)
        up[...] = dot(hot_t, ut[...].reshape(640, 512), ((1,), (1,))).astype(BF16)

    apply_end(0, img, own_u)
    b1 = s_ref[...] * inv_wide
    p = (dg[...] - wide(shift)) * b1 + img[...]
    vec[...] = p
    apply_start(1, p.astype(BF16))
    apply_end(1, img2)
    b1 = s_ref[...] * inv_wide
    p = vec[...]
    w = dg[...] * p + img2[...]
    sum_start(1, [column_sum(v) for v in (b1 * p, p * p, b1 * w, p * w, w * w)])
    img2[...] = w
    done = len(sends)
    for what in sends:
        drain(*what)
    sum_turn(1)
    e, pp, f, g, ww = sum_end(1, 5)
    h11 = e + shift * b1b1
    delta = h11 - shift
    h21 = jnp.sqrt(jnp.maximum(pp - 2.0 * delta * e + delta * delta * b1b1, 0.0) + EPSILON)
    inv_h21 = 1.0 / h21
    h12 = (f - delta * h11) * inv_h21
    h22 = (g - delta * (pp + shift * e + f - delta * h11)) * (inv_h21 * inv_h21)
    of_w = inv_h21
    of_p = -(delta + h22) * inv_h21
    of_b = -(delta * (shift - h22) * inv_h21 + h12)
    rest = (
        of_w * of_w * ww + of_p * of_p * pp + of_b * of_b * b1b1
        + 2.0 * (of_w * of_p * g + of_w * of_b * f + of_p * of_b * e)
    )
    inv_one = 1.0 / jnp.sqrt(h11 * h11 + h21 * h21)
    cos_one = h11 * inv_one
    sin_one = h21 * inv_one
    top = cos_one * h12 + sin_one * h22
    low = cos_one * h22 - sin_one * h12
    y_two = -low * sin_one * beta / (low * low + jnp.maximum(rest, 0.0) + EPSILON)
    y_one = (cos_one * beta - top * y_two) * inv_one
    of_one = beta - y_one * h11 - y_two * h12
    of_two = -(y_one * h21 + y_two * h22) * inv_h21
    y_over = y_two * inv_h21
    rows = (
        (y_one - y_over * delta) * inv_beta,
        y_over,
        (of_one - of_two * delta - y_two * of_b) * inv_beta,
        of_two - y_two * of_p,
        -y_over,
    )
    for ref, value in zip((c0, c1, c2, c3, c4), rows):
        ref[...] = wide(value)
    for what in sends[done:]:
        drain(*what)


def combine(rhs, vec, image, c0, c1, c2, c3, c4, sol_hbm, res_hbm, sol, res, sem):
    copies = []
    for k in range(4):
        part = pl.ds(k * 128, 128)
        r, v, m = rhs[part], vec[part], image[part]
        sol[part] = c0[...] * r + c1[...] * v
        copies.append(pltpu.make_async_copy(sol.at[part], sol_hbm.at[part], sem.at[0, k]))
        copies[-1].start()
        res[part] = c2[...] * r + c3[...] * v + c4[...] * m
        copies.append(pltpu.make_async_copy(res.at[part], res_hbm.at[part], sem.at[1, k]))
        copies[-1].start()
    for copy in copies:
        copy.wait()


def local(rhs, order, diag, blocks, near_rows, near_cols, gen_u, gen_v):
    vmem, hbm = (pl.BlockSpec(memory_space=m) for m in (pltpu.VMEM, pltpu.HBM))
    scratch = [
        ((512, 256), F32),
        ((12, BLK, BLK), BF16),
        ((5, 4, 2, 16, 512), BF16),
        ((5, 4, 2, 16, 512), BF16),
        ((4, 512, BLK), BF16),
        ((512, 512), BF16),
        ((640, 512), BF16),
        ((512, 640), BF16),
        ((512, 1536), BF16),
        ((1536, 256), BF16),
        ((640, 256), BF16),
        ((512, 256), F32),
        ((512, 256), F32),
        ((2, 16, 16, 128), BF16),
        ((2, 16, 32, 128), BF16),
        ((2, 8, 32, 128), BF16),
        ((2, 4, 64, 128), BF16),
        ((2, 16, 16, 128), BF16),
        ((2, 16, 32, 128), BF16),
        ((2, 8, 32, 128), BF16),
        ((2, 4, 64, 128), BF16),
        ((2, 48, 128), F32),
        ((2, 8, 16, 128), F32),
        ((2, 16, 128), BF16),
        ((2, 32, 128), BF16),
        ((2, 32, 128), BF16),
        ((2, 64, 128), BF16),
        ((2, 16, 16, 128), BF16),
        ((2, 16, 32, 128), BF16),
        ((2, 8, 32, 128), BF16),
        ((2, 4, 64, 128), BF16),
        ((12, BLK, 256), BF16),
        ((12, BLK, 256), BF16),
        ((2, 16, 128), F32),
        ((2, 16, 16, 128), F32),
        ((2, 16, 128), F32),
        ((2, 8, 16, 128), F32),
    ]
    vec, image, *coef = pl.pallas_call(
        kernel,
        out_shape=[jax.ShapeDtypeStruct(shape, F32) for shape in (rhs.shape,) * 2 + ((1, 256),) * 5],
        in_specs=[hbm] * 8,
        out_specs=[vmem] * 7,
        scratch_shapes=[pltpu.VMEM((1, 512), jnp.int32), pltpu.VMEM((1, 512), F32)]
        + [pltpu.SMEM((12,), jnp.int32)] * 2
        + [pltpu.VMEM(*s) for s in scratch] + [pltpu.SemaphoreType.DMA((72,))],
        compiler_params=pltpu.CompilerParams(
            collective_id=0, has_side_effects=True, vmem_limit_bytes=ROOM
        ),
    )(
        *(
            pltpu.with_memory_space_constraint(value, pltpu.HBM)
            for value in (
                order.reshape(1, -1), diag.reshape(1, -1), near_rows, near_cols, rhs, blocks,
                gen_u.transpose(0, 2, 1).reshape(5, 2, 16, -1), gen_v.transpose(0, 2, 1).reshape(5, 2, 16, -1),
            )
        )
    )
    return pl.pallas_call(
        combine,
        out_shape=[jax.ShapeDtypeStruct(rhs.shape, F32)] * 2,
        in_specs=[vmem] * 8,
        out_specs=[hbm] * 2,
        scratch_shapes=[pltpu.VMEM((512, 256), F32)] * 2 + [pltpu.SemaphoreType.DMA((2, 4))],
        compiler_params=pltpu.CompilerParams(vmem_limit_bytes=LAST),
    )(rhs, vec, image, *coef)


def solution(mesh):
    in_specs = (
        P(("leaf", "rank"), "rhs"),
        P(("leaf", "rank")),
        P(("leaf", "rank")),
        P(("leaf", "rank"), None, None),
        P(("leaf", "rank")),
        P(("leaf", "rank")),
        P(None, "leaf", "rank"),
        P(None, "leaf", "rank"),
    )
    out_specs = (P(("leaf", "rank"), "rhs"), P(("leaf", "rank"), "rhs"))
    return jax.shard_map(local, mesh=mesh, in_specs=in_specs, out_specs=out_specs, check_vma=False)
```

```python
import functools

import jax
import jax.numpy as jnp
from jax import lax
from jax.experimental import pallas as pl
from jax.experimental.pallas import tpu as pltpu
from jax.sharding import PartitionSpec as P

EPSILON = 1e-06
MESH = pl.DeviceIdType.MESH
F32, BF16 = jnp.float32, jnp.bfloat16
BLK = 128
KEEP = 128
ROOM, LAST = 40_000_000, 8_000_000
HOPS = (0, 1, 2, 1)
PLANE = [(dy, dx) for dy in range(4) for dx in range(4)]
FAR = sorted(range(1, 16), key=lambda d: -HOPS[d // 4] - HOPS[d % 4])
FAR_Z = (4, 5, 7, 3, 6, 2, 1)


def flip(value, bit):
    return value + bit - 2 * bit * lax.rem(lax.div(value, bit), 2)


def dot(a, b, contract=((1,), (0,))):
    return lax.dot_general(a, b, (contract, ((), ())), preferred_element_type=F32)


def kernel(
    order_hbm, diag_hbm, rows_hbm, cols_hbm, rhs_hbm, blocks_hbm, gu_hbm, gv_hbm, vec, img2, c0, c1, c2, c3, c4,
    order_ref, diag_ref, rows_ref, cols_ref, s_ref, blk, vt, ut, pt, pm, vp, up, bm, xg, cs, dg, img,
    sb4, sb, l1b, l0b, r4, r24, r1, r0, zs, zr, g4, g24, g1, g0, cf4, cf24, cf1, cf0, ext0, ext1, ps, pr, pz, pzr,
    sem,
):
    leaf, y, core = (lax.axis_index(name) for name in ("leaf", "rank", "rhs"))
    x, z = lax.rem(leaf, 4), lax.div(leaf, 4)
    xs = [x, flip(x, 1), flip(x, 2), 3 - x]
    ys = [y] + [lax.rem(y + k, 4) for k in (1, 2, 3)]
    back = [y] + [lax.rem(y + 4 - k, 4) for k in (1, 2, 3)]
    zs_of = [z]
    for bit in (1, 2, 4):
        zs_of = zs_of + [flip(v, bit) for v in zs_of]
    slot = y * 4 + x
    slot1 = y * 2 + lax.rem(x, 2)
    twin = (leaf, y, 1 - core)
    sends = []

    def plane_id(dy, dx):
        return (z * 4 + xs[dx], ys[dy], core)

    def column_id(dz):
        return (zs_of[dz] * 4 + x, y, core)

    def remote(src, dst, send, recv, to):
        return pltpu.make_async_remote_copy(
            src_ref=src, dst_ref=dst, send_sem=send, recv_sem=recv, device_id=to, device_id_type=MESH
        )

    def push(*what):
        remote(*what).start()

    taken = []

    def fresh(count):
        first = len(taken)
        taken.extend(range(count))
        return [sem.at[first + k] for k in range(count)]

    def drain(ref, done):
        pltpu.make_async_copy(ref, ref, done).wait()

    barrier = pltpu.get_barrier_semaphore()
    peers = [plane_id(dy, dx) for dy, dx in PLANE[1:]] + [column_id(dz) for dz in range(1, 8)] + [twin]
    for peer in peers:
        pl.semaphore_signal(barrier, inc=1, device_id=peer, device_id_type=MESH)

    own_cols = pl.ds(pl.multiple_of(y * 512, 512), 512)
    pairs = (
        (order_hbm, order_ref), (diag_hbm, diag_ref), (rhs_hbm, s_ref), (rows_hbm, rows_ref), (cols_hbm, cols_ref),
        (blocks_hbm, blk), (gv_hbm.at[:, :, :, own_cols], vt.at[:, y]), (gu_hbm.at[:, :, :, own_cols], ut.at[:, y]),
    )
    loads = [pltpu.make_async_copy(src, dst, done) for (src, dst), done in zip(pairs, fresh(8))]
    for load in loads:
        load.start()
    load_o, load_d, load_s, load_r, load_c, load_b, load_v, load_u = loads

    load_o.wait()
    load_d.wait()
    ol = order_ref[...] - (leaf * 4 + y) * 512
    row = lax.broadcasted_iota(jnp.int32, (512, 512), 0)
    col = lax.broadcasted_iota(jnp.int32, (512, 512), 1)
    hit = row == ol
    dg[...] = jnp.broadcast_to(
        jnp.sum(jnp.where(hit, jnp.broadcast_to(diag_ref[...], (512, 512)), 0.0), axis=1, keepdims=True), (512, 256)
    )
    hot = jnp.where(hit, 1.0, 0.0).astype(BF16)
    for r in range(4):
        pt[r] = hot[:, r * BLK : (r + 1) * BLK]

    load_s.wait()
    s = s_ref[...]
    sq = s * s

    sum_sems = [fresh(4), fresh(4)]

    def sum_start(i, values):
        rows = [v[:, c * 128 : c * 128 + 128] for v in values for c in range(2)]
        ps[i, : len(rows)] = jnp.concatenate(rows, 0)
        part, (sent, got, _, _) = pl.ds(0, 4 + 6 * i), sum_sems[i]
        for d in FAR:
            push(ps.at[i, part], pr.at[i, d, part], sent, got, plane_id(*PLANE[d]))
        sends.append((pr.at[i, pl.ds(1, 15), part], sent))

    def sum_turn(i):
        part, (_, got, sent, _) = pl.ds(0, 4 + 6 * i), sum_sems[i]
        drain(pr.at[i, pl.ds(1, 15), part], got)
        total = ps[i, part]
        for d in range(1, 16):
            total = total + pr[i, d, part]
        pz[i, part] = total
        for dz in FAR_Z:
            push(pz.at[i, part], pzr.at[i, dz, part], sent, sum_sems[i][3], column_id(dz))
        sends.append((pzr.at[i, pl.ds(1, 7), part], sent))

    def sum_end(i, count):
        part = pl.ds(0, 4 + 6 * i)
        drain(pzr.at[i, pl.ds(1, 7), part], sum_sems[i][3])
        total = pz[i, part]
        for dz in range(1, 8):
            total = total + pzr[i, dz, part]
        return [total[2 * k : 2 * k + 2] for k in range(count)]

    def wide(value):
        return jnp.concatenate([value[0:1], value[1:2]], 1)

    def column_sum(value):
        return jnp.sum(value, axis=0, keepdims=True)

    ps[...] = jnp.zeros_like(ps)
    first = [column_sum(sq), column_sum(dg[...] * sq)]
    pl.semaphore_wait(barrier, len(peers))

    v_sems, u_sems = fresh(6), fresh(6)

    def spread(gen, held, sems):
        for k, dy in enumerate((1, 3, 2)):
            columns = pl.ds(pl.multiple_of(ys[dy] * 512, 512), 512)
            push(gen.at[:, core, :, columns], held.at[:, y, core], sems[3], sems[k], plane_id(dy, 0))
        sends.append((held.at[:, pl.ds(0, 3), core], sems[3]))

    def hand_on(gen, held, sems):
        for k, dy in enumerate((1, 3, 2)):
            mine = held.at[:, back[dy], core]
            drain(mine, sems[k])
            push(mine, mine, sems[4], sems[5], twin)
        sends.append((held.at[:, pl.ds(0, 3), core], sems[4]))

    def gathered(held, sems):
        drain(held.at[:, pl.ds(0, 3), 1 - core], sems[5])

    sum_start(0, first)
    spread(gv_hbm, vt, v_sems)

    eye = jnp.where(row == col, 1.0, 0.0).astype(BF16)
    pm[...] = dot(eye, hot, ((1,), (1,))).astype(BF16)
    load_b.wait()
    load_r.wait()
    load_c.wait()
    for k in range(12):
        at = jnp.clip(rows_ref[k] - (leaf * 4 + y) * 4, 0, 3)
        bm[:, k * BLK : (k + 1) * BLK] = dot(pt[at], blk[k]).astype(BF16)
    sum_turn(0)
    hand_on(gv_hbm, vt, v_sems)
    spread(gu_hbm, ut, u_sems)
    load_v.wait()
    gathered(vt, v_sems)
    vp[...] = dot(vt[...].reshape(640, 512), hot, ((1,), (1,))).astype(BF16)

    s_sum, d_sum = sum_end(0, 2)
    beta = jnp.sqrt(s_sum + EPSILON)
    inv_beta = 1.0 / beta
    inv_wide = wide(inv_beta)
    shift = d_sum / (beta * beta)
    b1b1 = s_sum / (beta * beta)

    stage_sems = [[fresh(2) for _ in range(11)] for _ in range(2)]

    def apply_start(a, q):
        four, pair, zero, one, _, _, _, _, _, _, near = stage_sems[a]
        ext = (ext0, ext1)[a]
        ct = dot(vp[4 * KEEP :], q).astype(BF16)
        for t in range(16):
            g, c = t // 2, t % 2
            sb4[a, t] = ct[g * 16 :, c * 128 :][:16, :128]
        for d in FAR:
            dy, dx = PLANE[d]
            push(sb4.at[a, ys[dy] * 4 + xs[dx]], r4.at[a, d], *four, plane_id(dy, dx))
        sends.append((r4.at[a, pl.ds(1, 15)], four[0]))
        ct = dot(vp[: 4 * KEEP], q).astype(BF16)
        for t in range(16):
            g, c = t // 2, t % 2
            for b in range(2):
                sb[a, t, b * 16 : b * 16 + 16] = ct[(b + 2) * KEEP + g * 16 :, c * 128 :][:16, :128]
        for d in FAR:
            dy, dx = PLANE[d]
            push(sb.at[a, ys[dy] * 4 + xs[dx]], r24.at[a, d], *pair, plane_id(dy, dx))
        sends.append((r24.at[a, pl.ds(1, 15)], pair[0]))
        for t in range(4):
            for c in range(2):
                l0b[a, t, c * 32 : c * 32 + 32] = ct[t * 32 :, c * 128 :][:32, :128]
        for dy in range(4):
            push(l0b.at[a, ys[dy]], r0.at[a, dy], *zero, plane_id(dy, 1))
        sends.append((r0.at[a], zero[0]))
        for t in range(8):
            for c in range(2):
                l1b[a, t, c * 16 : c * 16 + 16] = ct[KEEP + t * 16 :, c * 128 :][:16, :128]
        for dy in range(4):
            for dx in (2, 3):
                there = ys[dy] * 2 + lax.rem(xs[dx], 2)
                push(l1b.at[a, there], r1.at[a, dy * 2 + dx - 2], *one, plane_id(dy, dx))
        sends.append((r1.at[a], one[0]))
        ext[4:8] = dot(pm[...], q).astype(BF16).reshape(4, BLK, 256)
        push(ext.at[pl.ds(4, 4)], ext.at[pl.ds(0, 4)], *near, plane_id(1, 0))
        push(ext.at[pl.ds(4, 4)], ext.at[pl.ds(8, 4)], *near, plane_id(3, 0))
        sends.append((ext.at[pl.ds(0, 8)], near[0]))

    def apply_end(a, out, before=None):
        ext = (ext0, ext1)[a]
        four, pair, zero, one, z_four, z_pair, all_four, all_pair, all_zero, all_one, near = stage_sems[a]

        def push_z(dz, pair_of):
            b = 0 if dz < 2 else 1 if dz < 4 else 2
            push(zs.at[a, pl.ds(b * 16, 16)], zr.at[a, dz], *pair_of, column_id(dz))

        drain(r4.at[a, pl.ds(1, 15)], four[1])
        total = sb4[a, slot].astype(F32)
        for d in range(1, 16):
            total = total + r4[a, d].astype(F32)
        zs[a, 32:48] = total
        for dz in (4, 5, 7, 6):
            push_z(dz, z_four)
        drain(r24.at[a, pl.ds(1, 15)], pair[1])
        total = sb[a, slot].astype(F32)
        for d in range(1, 16):
            total = total + r24[a, d].astype(F32)
        zs[a, 0:32] = total
        for dz in (3, 2, 1):
            push_z(dz, z_pair)
        sends.append((zr.at[a, pl.ds(4, 4)], z_four[0]))
        sends.append((zr.at[a, pl.ds(1, 3)], z_pair[0]))

        drain(r0.at[a], zero[1])
        total = jnp.zeros((64, 128), F32)
        for dy in range(4):
            total = total + r0[a, dy].astype(F32)
        g0[a] = total.astype(BF16)
        for dy in (2, 1, 3):
            push(g0.at[a], cf0.at[a, y], *all_zero, plane_id(dy, 0))
        cf0[a, y] = g0[a]
        sends.append((cf0.at[a, pl.ds(0, 3)], all_zero[0]))
        drain(r1.at[a], one[1])
        total = jnp.zeros((32, 128), F32)
        for k in range(8):
            total = total + r1[a, k].astype(F32)
        g1[a] = total.astype(BF16)
        for dy in (2, 1, 3, 0):
            for dx in (1, 0):
                if dy or dx:
                    push(g1.at[a], cf1.at[a, slot1], *all_one, plane_id(dy, dx))
        cf1[a, slot1] = g1[a]
        sends.append((cf1.at[a, pl.ds(0, 7)], all_one[0]))

        drain(zr.at[a, pl.ds(4, 4)], z_four[1])
        g4[a] = (zr[a, 4] + zr[a, 5] + zr[a, 6] + zr[a, 7]).astype(BF16)
        for d in FAR:
            push(g4.at[a], cf4.at[a, slot], *all_four, plane_id(*PLANE[d]))
        sends.append((cf4.at[a, pl.ds(0, 15)], all_four[0]))
        drain(zr.at[a, pl.ds(1, 3)], z_pair[1])
        g24[a, 0:16] = zr[a, 1].astype(BF16)
        g24[a, 16:32] = (zr[a, 2] + zr[a, 3]).astype(BF16)
        for d in FAR:
            push(g24.at[a], cf24.at[a, slot], *all_pair, plane_id(*PLANE[d]))
        sends.append((cf24.at[a, pl.ds(0, 15)], all_pair[0]))
        cf4[a, slot] = g4[a]
        cf24[a, slot] = g24[a]

        if before is not None:
            before()
        drain(ext.at[pl.ds(0, 8)], near[1])
        for k in range(12):
            at = jnp.clip(cols_ref[k] - (leaf * 4 + y) * 4 + 4, 0, 11)
            xg[k * BLK : (k + 1) * BLK] = ext[at]
        out[...] = dot(bm[...], xg[...])

        drain(cf0.at[a, pl.ds(0, 3)], all_zero[1])
        for t in range(4):
            for c in range(2):
                cs[t * 32 : t * 32 + 32, c * 128 : c * 128 + 128] = cf0[a, t, c * 32 : c * 32 + 32]
        drain(cf1.at[a, pl.ds(0, 7)], all_one[1])
        for t in range(8):
            for c in range(2):
                cs[KEEP + t * 16 : KEEP + t * 16 + 16, c * 128 : c * 128 + 128] = cf1[a, t, c * 16 : c * 16 + 16]
        out[...] += dot(up[:, : 2 * KEEP], cs[: 2 * KEEP])
        drain(cf4.at[a, pl.ds(0, 15)], all_four[1])
        for t in range(16):
            g, c = t // 2, t % 2
            at = 4 * KEEP + g * 16
            cs[at : at + 16, c * 128 : c * 128 + 128] = cf4[a, t]
        out[...] += dot(up[:, 4 * KEEP :], cs[4 * KEEP :])
        drain(cf24.at[a, pl.ds(0, 15)], all_pair[1])
        for t in range(16):
            g, c = t // 2, t % 2
            for b in range(2):
                at = (b + 2) * KEEP + g * 16
                cs[at : at + 16, c * 128 : c * 128 + 128] = cf24[a, t, b * 16 : b * 16 + 16]
        out[...] += dot(up[:, 2 * KEEP : 4 * KEEP], cs[2 * KEEP : 4 * KEEP])

    b1 = s * inv_wide
    apply_start(0, b1.astype(BF16))

    def own_u():
        load_u.wait()
        hand_on(gu_hbm, ut, u_sems)
        gathered(ut, u_sems)
        hot_t = jnp.concatenate([pt[r] for r in range(4)], 1)
        up[...] = dot(hot_t, ut[...].reshape(640, 512), ((1,), (1,))).astype(BF16)

    apply_end(0, img, own_u)
    b1 = s_ref[...] * inv_wide
    p = (dg[...] - wide(shift)) * b1 + img[...]
    vec[...] = p
    apply_start(1, p.astype(BF16))
    apply_end(1, img2)
    b1 = s_ref[...] * inv_wide
    p = vec[...]
    w = dg[...] * p + img2[...]
    sum_start(1, [column_sum(v) for v in (b1 * p, p * p, b1 * w, p * w, w * w)])
    img2[...] = w
    done = len(sends)
    for what in sends:
        drain(*what)
    sum_turn(1)
    e, pp, f, g, ww = sum_end(1, 5)
    h11 = e + shift * b1b1
    delta = h11 - shift
    h21 = jnp.sqrt(jnp.maximum(pp - 2.0 * delta * e + delta * delta * b1b1, 0.0) + EPSILON)
    inv_h21 = 1.0 / h21
    h12 = (f - delta * h11) * inv_h21
    h22 = (g - delta * (pp + shift * e + f - delta * h11)) * (inv_h21 * inv_h21)
    of_w = inv_h21
    of_p = -(delta + h22) * inv_h21
    of_b = -(delta * (shift - h22) * inv_h21 + h12)
    rest = (
        of_w * of_w * ww + of_p * of_p * pp + of_b * of_b * b1b1
        + 2.0 * (of_w * of_p * g + of_w * of_b * f + of_p * of_b * e)
    )
    inv_one = 1.0 / jnp.sqrt(h11 * h11 + h21 * h21)
    cos_one = h11 * inv_one
    sin_one = h21 * inv_one
    top = cos_one * h12 + sin_one * h22
    low = cos_one * h22 - sin_one * h12
    y_two = -low * sin_one * beta / (low * low + jnp.maximum(rest, 0.0) + EPSILON)
    y_one = (cos_one * beta - top * y_two) * inv_one
    of_one = beta - y_one * h11 - y_two * h12
    of_two = -(y_one * h21 + y_two * h22) * inv_h21
    y_over = y_two * inv_h21
    rows = (
        (y_one - y_over * delta) * inv_beta,
        y_over,
        (of_one - of_two * delta - y_two * of_b) * inv_beta,
        of_two - y_two * of_p,
        -y_over,
    )
    for ref, value in zip((c0, c1, c2, c3, c4), rows):
        ref[...] = wide(value)
    for what in sends[done:]:
        drain(*what)


def combine(rhs, vec, image, c0, c1, c2, c3, c4, sol_hbm, res_hbm, sol, res, sem):
    copies = []
    for k in range(4):
        part = pl.ds(k * 128, 128)
        r, v, m = rhs[part], vec[part], image[part]
        sol[part] = c0[...] * r + c1[...] * v
        copies.append(pltpu.make_async_copy(sol.at[part], sol_hbm.at[part], sem.at[0, k]))
        copies[-1].start()
        res[part] = c2[...] * r + c3[...] * v + c4[...] * m
        copies.append(pltpu.make_async_copy(res.at[part], res_hbm.at[part], sem.at[1, k]))
        copies[-1].start()
    for copy in copies:
        copy.wait()


def local(rhs, order, diag, blocks, near_rows, near_cols, gen_u, gen_v):
    vmem, hbm = (pl.BlockSpec(memory_space=m) for m in (pltpu.VMEM, pltpu.HBM))
    scratch = [
        ((512, 256), F32),
        ((12, BLK, BLK), BF16),
        ((5, 4, 2, 16, 512), BF16),
        ((5, 4, 2, 16, 512), BF16),
        ((4, 512, BLK), BF16),
        ((512, 512), BF16),
        ((640, 512), BF16),
        ((512, 640), BF16),
        ((512, 1536), BF16),
        ((1536, 256), BF16),
        ((640, 256), BF16),
        ((512, 256), F32),
        ((512, 256), F32),
        ((2, 16, 16, 128), BF16),
        ((2, 16, 32, 128), BF16),
        ((2, 8, 32, 128), BF16),
        ((2, 4, 64, 128), BF16),
        ((2, 16, 16, 128), BF16),
        ((2, 16, 32, 128), BF16),
        ((2, 8, 32, 128), BF16),
        ((2, 4, 64, 128), BF16),
        ((2, 48, 128), F32),
        ((2, 8, 16, 128), F32),
        ((2, 16, 128), BF16),
        ((2, 32, 128), BF16),
        ((2, 32, 128), BF16),
        ((2, 64, 128), BF16),
        ((2, 16, 16, 128), BF16),
        ((2, 16, 32, 128), BF16),
        ((2, 8, 32, 128), BF16),
        ((2, 4, 64, 128), BF16),
        ((12, BLK, 256), BF16),
        ((12, BLK, 256), BF16),
        ((2, 16, 128), F32),
        ((2, 16, 16, 128), F32),
        ((2, 16, 128), F32),
        ((2, 8, 16, 128), F32),
    ]
    vec, image, *coef = pl.pallas_call(
        kernel,
        out_shape=[jax.ShapeDtypeStruct(shape, F32) for shape in (rhs.shape,) * 2 + ((1, 256),) * 5],
        in_specs=[hbm] * 8,
        out_specs=[vmem] * 7,
        scratch_shapes=[pltpu.VMEM((1, 512), jnp.int32), pltpu.VMEM((1, 512), F32)]
        + [pltpu.SMEM((12,), jnp.int32)] * 2
        + [pltpu.VMEM(*s) for s in scratch] + [pltpu.SemaphoreType.DMA((72,))],
        compiler_params=pltpu.CompilerParams(
            collective_id=0, has_side_effects=True, vmem_limit_bytes=ROOM
        ),
    )(
        *(
            pltpu.with_memory_space_constraint(value, pltpu.HBM)
            for value in (
                order.reshape(1, -1), diag.reshape(1, -1), near_rows, near_cols, rhs, blocks,
                gen_u.transpose(0, 2, 1).reshape(5, 2, 16, -1), gen_v.transpose(0, 2, 1).reshape(5, 2, 16, -1),
            )
        )
    )
    return pl.pallas_call(
        combine,
        out_shape=[jax.ShapeDtypeStruct(rhs.shape, F32)] * 2,
        in_specs=[vmem] * 8,
        out_specs=[hbm] * 2,
        scratch_shapes=[pltpu.VMEM((512, 256), F32)] * 2 + [pltpu.SemaphoreType.DMA((2, 4))],
        compiler_params=pltpu.CompilerParams(vmem_limit_bytes=LAST),
    )(rhs, vec, image, *coef)


def solution(mesh):
    in_specs = (
        P(("leaf", "rank"), "rhs"),
        P(("leaf", "rank")),
        P(("leaf", "rank")),
        P(("leaf", "rank"), None, None),
        P(("leaf", "rank")),
        P(("leaf", "rank")),
        P(None, "leaf", "rank"),
        P(None, "leaf", "rank"),
    )
    out_specs = (P(("leaf", "rank"), "rhs"), P(("leaf", "rank"), "rhs"))
    return jax.shard_map(local, mesh=mesh, in_specs=in_specs, out_specs=out_specs, check_vma=False)
```
